32 devices in a mesh: shot: 2 (over x), gy: 16 (over z, y, core).
Axes of the slice: x: 2, y: 2, z: 4, core: 2. Of those that a mesh axis runs over, the one named last changes fastest.
Arguments:
- source_now: float32 [32, 128, 256], P('shot', 'gy'), parts along dimension 0, may hold values from -4 to 4
- source_before: float32 [32, 128, 256], P('shot', 'gy'), parts along dimension 0, may hold values from -4 to 4
- receiver_now: float32 [32, 128, 256], P('shot', 'gy'), parts along dimension 0, may hold values from -4 to 4
- receiver_before: float32 [32, 128, 256], P('shot', 'gy'), parts along dimension 0, may hold values from -4 to 4
- speed_term: float32 [16, 128, 256], P(None, 'gy'), may hold values from 0.03 to 0.12
- aniso_field: float32 [16, 128, 256], P(None, 'gy'), may hold values from 0 to 0.3
- tilt_field: float32 [16, 128, 256], P(None, 'gy'), may hold values from -0.5 to 0.5
- angle_bins: int32 [16, 128, 256], P(None, 'gy'), may hold values from 0 to 7
- weight_table: bfloat16 [24, 8, 4], replicated, may hold values from -1.25 to 1.25
- offset_lags: int32 [24], replicated, may hold values from -16 to 16, as said below
- source_cells: int32 [16], P('shot'), parts along dimension 0, may hold values from 0 to 32767
- source_wavelet: float32 [4, 8], P('shot'), parts along dimension 0, may hold values from -24 to 24
- receiver_cells: int32 [4096], P('shot'), parts along dimension 0, may hold values from 0 to 32767
- receiver_traces: float32 [4, 2048], P('shot'), parts along dimension 0, may hold values from -18 to 18
Outputs:
- angle_images: bfloat16 [8, 16, 128, 256], P('shot', None, 'gy'), parts along dimension 0
The draws below stay inside these ranges and needn't reach their ends.
There are 2 independent parts, one for each index of `shot`. The reference program is written for one: setup_inputs(seed, part) draws one part's arguments, and reference() takes and returns one part's arrays. A program takes and returns all parts, laid end to end along the dimension named above; an argument that names none is the same for every part. Nothing has to cross between parts.
Inputs may be any that keep to these rules, and one draw needn't show every extreme that they name: `offset_lags`: 24 distinct lags; -16 and 16 are among them.
All inputs are finite; a program needn't handle non-finite values.
Results may differ from the reference program's by a relative error of at most 0.0051.
Values may be sent and summed in bfloat16 or wider, within the bound.
No kernel may reach another device: no remote copies, remote signals or barrier semaphores. Data moves between devices by JAX's collectives and lax.ppermute only.
A program may use at most 64 MiB of HBM per device.

```python
import math
import jax
import jax.numpy as jnp
from jax import lax

NX = 256
CY = 8
Z = 16
ITERS = 2
NOFF = 24
NANG = 4
NBIN = 8
NSRC = 8
NREC = 2048
NY = 128
LMAX = 16


def draw_offset_lags(key, part):
    reach = 2 * CY
    inner = jax.random.permutation(jax.random.fold_in(key, 11), 2 * reach - 1) - (reach - 1)
    chosen = jnp.concatenate([jnp.array([-reach, reach], jnp.int32), inner[:NOFF - 2].astype(jnp.int32)])
    return jax.random.permutation(jax.random.fold_in(key, 12), chosen)


def with_ends(drawn, stream_key, least, high):
    longest = drawn.shape.index(max(drawn.shape))
    spots = []
    for shift in (0, 1):
        where = [jax.random.randint(jax.random.fold_in(stream_key, axis), (), 0, length) for axis, length in enumerate(drawn.shape)]
        where[longest] = (where[longest] + shift) % drawn.shape[longest]
        spots.append(tuple(where))
    return drawn.at[spots[0]].set(least).at[spots[1]].set(high)


def shard_levels(key, extent, split, smallest, top_value):
    gain = 1.0
    for position, shards_of in split:
        steps = jax.random.uniform(jax.random.fold_in(jax.random.fold_in(key, 6), position), (shards_of,), jnp.float32, smallest / len(split), top_value / len(split))
        gain = gain * jnp.repeat(jnp.exp(steps), extent[position] // shards_of).reshape((-1,) + (1,) * (len(extent) - 1 - position))
    return gain


def noise(rng, extent, deviation, most, shards=(), held_as=jnp.bfloat16):
    factor_of = shard_levels(rng, extent, shards, -0.22, 0.18) if shards else 1.0
    values = jax.random.normal(rng, extent, jnp.float32) * deviation * factor_of
    return jnp.minimum(jnp.maximum(values, -most), most).astype(held_as)


def setup_inputs(seed: int = 0, part: int = 0) -> dict:
    key_of = jax.random.split(jax.random.key(seed), 15)
    own_keys = jax.random.split(jax.random.fold_in(key_of[14], part), 15)
    return {
        "source_now": noise(own_keys[0], (Z, NY, NX), 0.5, 4.0, ((1, 16),), jnp.float32),
        "source_before": noise(own_keys[1], (Z, NY, NX), 0.5, 4.0, ((1, 16),), jnp.float32),
        "receiver_now": noise(own_keys[2], (Z, NY, NX), 0.5, 4.0, ((1, 16),), jnp.float32),
        "receiver_before": noise(own_keys[3], (Z, NY, NX), 0.5, 4.0, ((1, 16),), jnp.float32),
        "speed_term": jnp.clip(jnp.exp(math.log(0.12) - 1.3862944 * jax.random.uniform(key_of[4], (Z, NY, NX), jnp.float32) ** shard_levels(key_of[4], (Z, NY, NX), ((1, 16),), -0.2, 0.2)), 0.03, 0.12),
        "aniso_field": jnp.clip(0.3 * jax.random.uniform(key_of[5], (Z, NY, NX), jnp.float32) ** shard_levels(key_of[5], (Z, NY, NX), ((1, 16),), -0.2, 0.2), 0.0, 0.3),
        "tilt_field": jnp.clip(jax.random.uniform(key_of[6], (Z, NY, NX), jnp.float32, -0.5, 0.5) * shard_levels(key_of[6], (Z, NY, NX), ((1, 16),), -0.4, 0.0), -0.5, 0.5),
        "angle_bins": with_ends(jax.random.randint(key_of[7], (Z, NY, NX), 0, NBIN), jax.random.fold_in(key_of[7], 1), 0, NBIN - 1).astype(jnp.int32),
        "weight_table": noise(key_of[8], (NOFF, NBIN, NANG), NOFF ** -0.5, 1.25),
        "offset_lags": draw_offset_lags(jax.random.fold_in(key_of[14], 71), part),
        "source_cells": with_ends(jax.random.randint(own_keys[10], (NSRC,), 0, NX * NY), jax.random.fold_in(own_keys[10], 1), 0, (NX * NY) - 1).astype(jnp.int32),
        "source_wavelet": noise(own_keys[11], (ITERS, NSRC), 4.0, 24.0, (), jnp.float32),
        "receiver_cells": with_ends(jax.random.randint(own_keys[12], (NREC,), 0, NX * NY), jax.random.fold_in(own_keys[12], 1), 0, (NX * NY) - 1).astype(jnp.int32),
        "receiver_traces": noise(own_keys[13], (ITERS, NREC), 3.0, 18.0, (), jnp.float32),
    }


SECOND_COEF = (-205.0 / 72.0, 8.0 / 5.0, -1.0 / 5.0, 8.0 / 315.0, -1.0 / 560.0)
FIRST_COEF = (4.0 / 5.0, -1.0 / 5.0, 4.0 / 105.0, -1.0 / 280.0)


def derivs(padded, dimension, length):
    middle = lax.slice_in_dim(padded, 4, 4 + length, axis=dimension)
    second = SECOND_COEF[0] * middle
    first_deriv = jnp.zeros_like(middle)
    for distance in range(1, 5):
        above_cells = lax.slice_in_dim(padded, 4 + distance, 4 + distance + length, axis=dimension)
        below_cells = lax.slice_in_dim(padded, 4 - distance, 4 - distance + length, axis=dimension)
        second = second + SECOND_COEF[distance] * (above_cells + below_cells)
        first_deriv = first_deriv + FIRST_COEF[distance - 1] * (above_cells - below_cells)
    return second, first_deriv


def pad_axis(array_in, dimension):
    widths = [(0, 0)] * array_in.ndim
    widths[dimension] = (4, 4)
    return jnp.pad(array_in, widths)


def operate(extended, aniso_field, tilt_field):
    row_count = extended.shape[2] - 8
    core_part = extended[:, :, 4:4 + row_count, :]
    second_y, first_y = derivs(extended, 2, row_count)
    second_x, first_x = derivs(pad_axis(core_part, 3), 3, core_part.shape[3])
    second_z, unused = derivs(pad_axis(core_part, 1), 1, core_part.shape[1])
    unused_two, mixed_term = derivs(pad_axis(first_x + first_y, 1), 1, core_part.shape[1])
    return (1.0 + 2.0 * aniso_field) * (second_x + second_y) + second_z + tilt_field * mixed_term


def inject(fields, step_index, positions, amounts, member, grid_width, first_row):
    row_local = positions // grid_width - first_row
    inside = (row_local >= 0) & (row_local < fields.shape[2])
    clipped = jnp.clip(row_local, 0, fields.shape[2] - 1)
    added = jnp.where(inside, amounts[step_index], jnp.zeros_like(amounts[step_index]))
    return fields.at[member, 0, clipped, positions % grid_width].add(added)


def lag_products(source_win, receiver_win, offset_lags, center, row_count):
    def single(lag_value):
        source_part = lax.dynamic_slice_in_dim(source_win, center - lag_value, row_count, 1).astype(jnp.float32)
        receiver_part = lax.dynamic_slice_in_dim(receiver_win, center + lag_value, row_count, 1).astype(jnp.float32)
        return (source_part * receiver_part).reshape(-1)
    return jax.vmap(single)(offset_lags)


def combine(products, bin_ids, weights):
    flat_weights = weights.astype(jnp.float32).reshape(weights.shape[0], -1)
    mixed_term = jnp.dot(flat_weights.T, products, precision=lax.Precision.HIGHEST, preferred_element_type=jnp.float32)
    mixed_term = mixed_term.reshape(weights.shape[1], weights.shape[2], -1)
    chosen = (bin_ids[None, :] == jnp.arange(weights.shape[1], dtype=jnp.int32)[:, None]).astype(jnp.float32)
    return jnp.sum(chosen[:, None, :] * mixed_term, axis=0)


def reference(source_now, source_before, receiver_now, receiver_before, speed_term, aniso_field, tilt_field, angle_bins, weight_table, offset_lags, source_cells, source_wavelet, receiver_cells, receiver_traces):
    now_fields = jnp.stack([source_now, receiver_now])
    prev_fields = jnp.stack([source_before, receiver_before])
    image_sum = jnp.zeros((NANG, Z, NY, NX), jnp.float32)
    for step_index in range(ITERS):
        extended = jnp.pad(now_fields, ((0, 0), (0, 0), (4, 4), (0, 0)), mode="wrap")
        next_fields = 2.0 * now_fields - prev_fields + speed_term * operate(extended, aniso_field, tilt_field)
        next_fields = inject(next_fields, step_index, source_cells, source_wavelet, 0, NX, 0)
        next_fields = inject(next_fields, step_index, receiver_cells, receiver_traces, 1, NX, 0)
        prev_fields, now_fields = now_fields, next_fields
        rounded = now_fields.astype(jnp.bfloat16)
        padded = jnp.pad(rounded, ((0, 0), (0, 0), (LMAX, LMAX), (0, 0)), mode="wrap")
        moved = jnp.moveaxis(padded, 1, 0)

        def plane_image(pieces):
            planes, bin_plane = pieces
            products = lag_products(planes[0][None], planes[1][None], offset_lags, LMAX, NY)
            return combine(products, bin_plane.reshape(-1), weight_table).reshape(NANG, NY, NX)

        images = lax.map(plane_image, (moved, angle_bins))
        image_sum = image_sum + jnp.moveaxis(images, 0, 1)
    return image_sum.astype(jnp.bfloat16)
```

```python
import functools

import jax
import jax.numpy as jnp
from jax import lax
from jax.experimental import pallas as pl
from jax.experimental.pallas import tpu as pltpu
from jax.sharding import PartitionSpec as P

STEPS = 2
SECOND = (-205.0 / 72.0, 8.0 / 5.0, -1.0 / 5.0, 8.0 / 315.0, -1.0 / 560.0)
FIRST = (4.0 / 5.0, -1.0 / 5.0, 4.0 / 105.0, -1.0 / 280.0)
REACH = 4
LANES = 128
F32 = jnp.float32
BF16 = jnp.bfloat16

VMEM = pl.BlockSpec(memory_space=pltpu.VMEM)
SMEM = pl.BlockSpec(memory_space=pltpu.SMEM)


def call(kernel, outs, in_specs, scratch, mib, flops, bytes_moved):
    multiple = isinstance(outs, (list, tuple))
    return pl.pallas_call(
        kernel,
        out_shape=outs,
        in_specs=in_specs,
        out_specs=[VMEM] * len(outs) if multiple else VMEM,
        scratch_shapes=scratch,
        compiler_params=pltpu.CompilerParams(vmem_limit_bytes=mib << 20),
        cost_estimate=pl.CostEstimate(
            flops=flops, bytes_accessed=bytes_moved, transcendentals=0
        ),
    )


def is_odd():
    return lax.axis_index("gy") % 2 == 1


def sublane(shape):
    return lax.broadcasted_iota(jnp.int32, shape, len(shape) - 2)


def pack_kernel(sn, sb, rn, rb, sp, an, ti, out_x, out_s):
    depth, rows, width = sn.shape
    half = rows // 2
    full = depth * rows
    odd = is_odd()
    for place, field in enumerate((sn, rn)):
        value = field[...].reshape(full, width).astype(BF16)
        out_x[place * full : (place + 1) * full] = value
        out_s[place * full : (place + 1) * full] = value
    first_half = sublane((depth, rows, width)) < half

    def joined(a, b, start, count):
        keep = first_half[: a.shape[0]]
        turned_a = pltpu.roll(a, half, 1)
        turned_b = pltpu.roll(b, half, 1)
        low = jnp.where(keep, a, turned_b).reshape(count, width).astype(BF16)
        high = jnp.where(keep, turned_a, b).reshape(count, width).astype(BF16)
        out_x[start : start + count] = jnp.where(odd, high, low)
        out_s[start : start + count] = jnp.where(odd, low, high)

    joined(sb[...], rb[...], 2 * full, full)
    joined(sp[...], an[...], 3 * full, full)
    joined(ti[: depth // 2], ti[depth // 2 :], 4 * full, full // 2)


def inject_kernel(grid_rows, rc, rt, sc, sw, bins, inj, bins_y, onehot, left):
    count = rc.shape[1]
    depth, rows, width = bins.shape
    first_row = lax.axis_index("gy") * rows
    half = rows // 2
    shift = width.bit_length() - 1
    power = 1 << shift == width

    def row_of(cell):
        if power:
            return lax.shift_right_logical(cell, jnp.int32(shift))
        return lax.div(cell, jnp.int32(width))

    own = lax.broadcasted_iota(jnp.int32, (rows, 1), 0)
    own_row = first_row + own
    edge = first_row + jnp.where(own < half, own + rows, own - rows)
    edge_row = jnp.where(
        edge >= grid_rows, edge - grid_rows, jnp.where(edge < 0, edge + grid_rows, edge)
    )

    for start in range(0, count, LANES):
        cells = rc[:, start : start + LANES]
        at_row = row_of(cells)
        at_col = cells - at_row * width
        cols = lax.broadcasted_iota(jnp.int32, (width, LANES), 0)
        onehot[:, start : start + LANES] = jnp.where(cols == at_col, 1.0, 0.0).astype(BF16)
        parts = []
        for step, wanted in ((0, own_row), (0, edge_row), (1, own_row)):
            amount = rt[step : step + 1, start : start + LANES]
            coarse = amount.astype(BF16).astype(F32)
            fine = amount - coarse
            here = wanted == at_row
            parts.append(jnp.where(here, coarse, 0.0))
            parts.append(jnp.where(here, fine, 0.0))
        left[:, start : start + LANES] = jnp.concatenate(parts, 0).astype(BF16)
    spread = lax.dot_general(
        left[...], onehot[...], (((1,), (1,)), ((), ())), preferred_element_type=F32
    )
    cols = lax.broadcasted_iota(jnp.int32, (rows, width), 1)
    for place, (step, wanted) in enumerate(((0, own_row), (0, edge_row), (1, own_row))):
        base = 2 * place * rows
        inj[place, 1] = spread[base : base + rows] + spread[base + rows : base + 2 * rows]
        total = jnp.zeros((rows, width), F32)
        for i in range(sc.shape[0]):
            cell = sc[i]
            at_row = lax.div(cell, jnp.int32(width))
            at_col = cell - at_row * width
            here = jnp.logical_and(wanted == at_row, cols == at_col)
            total = total + jnp.where(here, sw[step, i], 0.0)
        inj[place, 0] = total
    for y in range(rows):
        bins_y[y] = bins[:, y, :]


def shifted_x(value, k, lane):
    width = value.shape[-1]
    above = jnp.where(lane < width - k, pltpu.roll(value, width - k, 1), 0.0)
    below = jnp.where(lane >= k, pltpu.roll(value, k, 1), 0.0)
    return above, below


def flat_terms(value, y_shifts, lane):
    second = (2.0 * SECOND[0]) * value
    first = None
    for k in range(1, REACH + 1):
        above, below = shifted_x(value, k, lane)
        up, down = y_shifts[k - 1]
        second = second + SECOND[k] * ((above + below) + (up + down))
        term = FIRST[k - 1] * ((above - below) + (up - down))
        first = term if first is None else first + term
    return second, first


def depth_terms(field, slope, at):
    second = SECOND[0] * field[at + REACH]
    first = None
    for k in range(1, REACH + 1):
        second = second + SECOND[k] * (field[at + REACH + k] + field[at + REACH - k])
        term = FIRST[k - 1] * (slope[at + REACH + k] - slope[at + REACH - k])
        first = term if first is None else first + term
    return second, first


def step_kernel(
    sn, sb, rn, rb, sp, an, ti, px, ps, inj, out,
    field, slope, base, edge_sp, edge_ti, later, later_edge, turned,
):
    depth, rows, width = sn.shape
    half = rows // 2
    full = depth * rows
    odd = is_odd()
    row = sublane((rows, width))
    lane = lax.broadcasted_iota(jnp.int32, (rows, width), 1)
    low_half = row < half
    now = (sn, rn)
    before = (sb, rb)

    zeros = jnp.zeros((REACH, rows, width), F32)
    for ref in (field, slope):
        for m in range(2):
            for t in range(2):
                ref[m, t, :REACH] = zeros
                ref[m, t, REACH + depth :] = zeros
    for m in range(2):
        later[m, :REACH] = zeros
        later[m, REACH + depth :] = zeros

    def from_packs(start):
        x = px[pl.ds(start, 2 * rows), :].astype(F32)
        s = ps[pl.ds(start, 2 * rows), :].astype(F32)
        return jnp.where(odd, s, x), jnp.where(odd, x, s)

    def roll(value, k):
        return pltpu.roll(value, k % rows, 0)

    def edge_pair(low, high):
        first = jnp.where(low_half, high, roll(low, half))
        second = jnp.where(low_half, roll(high, half), low)
        return first, second

    def tilt_edge(pair, c):
        start = pl.multiple_of(4 * full + pair * 2 * rows, 2 * rows)
        low2, high2 = from_packs(start)
        for j in range(2):
            part = slice(j * rows, (j + 1) * rows)
            a, b = edge_pair(low2[part], high2[part])
            edge_ti[2 * pair + j] = a
            edge_ti[2 * pair + j + depth // 2] = b
        return c

    lax.fori_loop(0, depth // 4, tilt_edge, 0, unroll=2)

    def flat(pair, c):
        offset = pair * 2 * rows
        starts = [pl.multiple_of(n * full + offset, 2 * rows) for n in range(4)]
        current = [from_packs(starts[m]) for m in range(2)]
        old_low, old_high = from_packs(starts[2])
        media_low, media_high = from_packs(starts[3])
        for j in range(2):
            part = slice(j * rows, (j + 1) * rows)
            z = 2 * pair + j
            old = edge_pair(old_low[part], old_high[part])
            speed_edge, aniso_edge = edge_pair(media_low[part], media_high[part])
            edge_sp[z] = speed_edge
            factor = (sp[z] * (1.0 + 2.0 * an[z]), speed_edge * (1.0 + 2.0 * aniso_edge))
            for m in range(2):
                low, high = current[m][0][part], current[m][1][part]
                mid = now[m][z]
                edge = jnp.where(low_half, high, low)
                own_shifts, edge_shifts = [], []
                for k in range(1, REACH + 1):
                    mid_up, mid_down = roll(mid, -k), roll(mid, k)
                    low_up, low_down = roll(low, -k), roll(low, k)
                    high_up, high_down = roll(high, -k), roll(high, k)
                    own_shifts.append(
                        (
                            jnp.where(row < rows - k, mid_up, high_up),
                            jnp.where(row >= k, mid_down, low_down),
                        )
                    )
                    edge_shifts.append(
                        (
                            jnp.where(
                                low_half, high_up, jnp.where(row < rows - k, low_up, mid_up)
                            ),
                            jnp.where(
                                low_half, jnp.where(row >= k, high_down, mid_down), low_down
                            ),
                        )
                    )
                for t, (value, shifts, prior) in enumerate(
                    ((mid, own_shifts, before[m][z]), (edge, edge_shifts, old[m]))
                ):
                    second, first = flat_terms(value, shifts, lane)
                    field[m, t, z + REACH] = value
                    slope[m, t, z + REACH] = first
                    base[m, t, z] = 2.0 * value - prior + factor[t] * second
        return c

    lax.fori_loop(0, depth // 2, flat, 0)

    def deep(z, c):
        speed = (sp[z], edge_sp[z])
        tilt = (ti[z], edge_ti[z])
        for m in range(2):
            for t in range(2):
                second, first = depth_terms(field.at[m, t], slope.at[m, t], z)
                value = base[m, t, z] + speed[t] * (second + tilt[t] * first)
                if t == 0:
                    later[m, z + REACH] = value
                else:
                    later_edge[m, z] = value
        return c

    lax.fori_loop(0, depth, deep, 0, unroll=2)
    for m in range(2):
        later[m, REACH] = later[m, REACH] + inj[0, m]
        later_edge[m, 0] = later_edge[m, 0] + inj[1, m]

    def flat_later(z, c):
        factor = sp[z] * (1.0 + 2.0 * an[z])
        for m in range(2):
            mid = later[m, z + REACH]
            edge = later_edge[m, z]
            shifts = []
            for k in range(1, REACH + 1):
                shifts.append(
                    (
                        jnp.where(row < rows - k, roll(mid, -k), roll(edge, -k)),
                        jnp.where(row >= k, roll(mid, k), roll(edge, k)),
                    )
                )
            second, first = flat_terms(mid, shifts, lane)
            slope[m, 0, z + REACH] = first
            base[m, 0, z] = 2.0 * mid - now[m][z] + factor * second
            for part in range(width // LANES):
                turned[0, m, part, pl.ds(z, rows, stride=depth), :] = mid[
                    :, part * LANES : (part + 1) * LANES
                ]
        return c

    lax.fori_loop(0, depth, flat_later, 0, unroll=2)

    def deep_later(z, c):
        surface = jnp.where(z == 0, 1.0, 0.0)
        for m in range(2):
            second, first = depth_terms(later.at[m], slope.at[m, 0], z)
            value = base[m, 0, z] + sp[z] * (second + ti[z] * first) + surface * inj[2, m]
            for part in range(width // LANES):
                turned[1, m, part, pl.ds(z, rows, stride=depth), :] = value[
                    :, part * LANES : (part + 1) * LANES
                ]
        return c

    lax.fori_loop(0, depth, deep_later, 0, unroll=2)
    for s in range(STEPS):
        for m in range(2):
            for part in range(width // LANES):
                for y in range(rows):
                    out[s, m, y, :, part * LANES : (part + 1) * LANES] = turned[
                        s, m, part, y * depth : (y + 1) * depth, :
                    ].astype(BF16)


def image_kernel(lags, far, near, own, chip, relay, bins, table, out, window, turned):
    rows, depth, width = bins.shape
    lag_count, angles = table.shape[:2]
    odd = jnp.where(is_odd(), 1, 0)
    for piece, place in ((far, 0), (near, 1), (own, 2), (chip, 3), (relay, 4)):
        block = (place + odd * (4 - 2 * place)) * rows
        for s in range(STEPS):
            for m in range(2):
                window[s, m, pl.ds(block, rows)] = piece[s, m].astype(F32)
    tiles = [(z, x) for z in range(0, depth, 8) for x in range(0, width, LANES)]

    def one_row(y, c):
        ids = bins[y]

        def one_lag(h, sums):
            lag = lags[h]
            at_s = y + 2 * rows - lag
            at_r = y + 2 * rows + lag
            sums = [list(a) for a in sums]
            for n, (z, x) in enumerate(tiles):
                zs, xs = slice(z, z + 8), slice(x, x + LANES)
                product = window[0, 0, at_s, zs, xs] * window[0, 1, at_r, zs, xs]
                for s in range(1, STEPS):
                    product = product + window[s, 0, at_s, zs, xs] * window[s, 1, at_r, zs, xs]
                for a in range(angles):
                    weight = jnp.take_along_axis(table[h, a], ids[zs, xs], axis=0)
                    sums[a][n] = sums[a][n] + weight * product
            return tuple(tuple(a) for a in sums)

        zero = jnp.zeros((8, LANES), F32)
        sums = lax.fori_loop(
            0, lag_count, one_lag, tuple((zero,) * len(tiles) for _ in range(angles)), unroll=4
        )
        for a in range(angles):
            for n, (z, x) in enumerate(tiles):
                turned[a, x // LANES, pl.ds(z * rows + y, 8, stride=rows), :] = sums[a][n]
        return c

    lax.fori_loop(0, rows, one_row, 0)
    for a in range(angles):
        for part in range(width // LANES):
            out[a, :, :, part * LANES : (part + 1) * LANES] = (
                turned[a, part].astype(BF16).reshape(depth, rows, LANES)
            )


def per_device(
    source_now, source_before, receiver_now, receiver_before, speed_term, aniso_field,
    tilt_field, angle_bins, weight_table, offset_lags, source_cells, source_wavelet,
    receiver_cells, receiver_traces,
):
    depth, rows, width = source_now.shape
    size = lax.axis_size("gy")
    full = depth * rows
    lag_count, bin_count, angles = weight_table.shape
    count = receiver_cells.shape[0]
    parts = width // LANES

    chip_route = [(i, i ^ 1) for i in range(size)]
    near_route = [(i, (i + 1 if i % 2 else i - 1) % size) for i in range(size)]
    far_route = [(i, (i - 2 if i % 2 else i + 2) % size) for i in range(size)]

    def moved(block, route):
        return lax.ppermute(block, "gy", route)

    fields = (
        source_now, source_before, receiver_now, receiver_before, speed_term, aniso_field,
        tilt_field,
    )
    pack_shape = jax.ShapeDtypeStruct((4 * full + full // 2, width), BF16)
    pack_x, pack_s = call(
        pack_kernel, [pack_shape] * 2, [VMEM] * 7, [], 8, full * width * 20, full * width * 40
    )(*fields)
    got_s = moved(pack_s, chip_route)
    got_x = moved(pack_x, near_route)

    inj, bins_y = call(
        functools.partial(inject_kernel, size * rows),
        [
            jax.ShapeDtypeStruct((3, 2, rows, width), F32),
            jax.ShapeDtypeStruct((rows, depth, width), jnp.int32),
        ],
        [VMEM, VMEM, SMEM, SMEM, VMEM],
        [pltpu.VMEM((width, count), BF16), pltpu.VMEM((6 * rows, count), BF16)],
        8,
        12 * rows * count * width,
        full * width * 8,
    )(receiver_cells[None], receiver_traces, source_cells, source_wavelet, angle_bins)
    table = jnp.broadcast_to(
        jnp.transpose(weight_table, (0, 2, 1)).astype(F32)[..., None],
        (lag_count, angles, bin_count, LANES),
    )

    padded = (2, 2, depth + 2 * REACH, rows, width)
    own = call(
        step_kernel,
        jax.ShapeDtypeStruct((STEPS, 2, rows, depth, width), BF16),
        [VMEM] * 10,
        [
            pltpu.VMEM(padded, F32),
            pltpu.VMEM(padded, F32),
            pltpu.VMEM((2, 2, depth, rows, width), F32),
            pltpu.VMEM((depth, rows, width), F32),
            pltpu.VMEM((depth, rows, width), F32),
            pltpu.VMEM((2, depth + 2 * REACH, rows, width), F32),
            pltpu.VMEM((2, depth, rows, width), F32),
            pltpu.VMEM((STEPS, 2, parts, full, LANES), F32),
        ],
        16,
        full * width * 600,
        full * width * 50,
    )(*fields, got_x, got_s, inj)

    far = moved(own, far_route)
    near = moved(own, near_route)
    chip = moved(own, chip_route)
    relay = moved(near, chip_route)
    return call(
        image_kernel,
        jax.ShapeDtypeStruct((angles, depth, rows, width), BF16),
        [SMEM] + [VMEM] * 7,
        [
            pltpu.VMEM((STEPS, 2, 5 * rows, depth, width), F32),
            pltpu.VMEM((angles, parts, full, LANES), F32),
        ],
        16,
        full * width * 24 * 12,
        full * width * 20,
    )(offset_lags, far, near, own, chip, relay, bins_y, table)


def solution(mesh):
    grid = P("shot", "gy", None)
    media = P(None, "gy", None)
    return jax.shard_map(
        per_device,
        mesh=mesh,
        in_specs=(grid,) * 4
        + (media,) * 4
        + (P(), P(), P("shot"), P("shot", None), P("shot"), P("shot", None)),
        out_specs=P("shot", None, "gy", None),
        check_vma=False,
    )
```

```python
import functools

import jax
import jax.numpy as jnp
from jax import lax
from jax.experimental import pallas as pl
from jax.experimental.pallas import tpu as pltpu
from jax.sharding import PartitionSpec as P


STEPS = 2
SECOND = (-205.0 / 72.0, 8.0 / 5.0, -1.0 / 5.0, 8.0 / 315.0, -1.0 / 560.0)
FIRST = (4.0 / 5.0, -1.0 / 5.0, 4.0 / 105.0, -1.0 / 280.0)
REACH = 4
LANES = 128
F32 = jnp.float32
BF16 = jnp.bfloat16

VMEM = pl.BlockSpec(memory_space=pltpu.VMEM)
HBM = pl.BlockSpec(memory_space=pltpu.HBM)


def in_hbm(arrays):
    return [pltpu.with_memory_space_constraint(array, pltpu.HBM) for array in arrays]


def fetch(sources, targets, sems):
    copies = [
        pltpu.make_async_copy(source, target, sems.at[n])
        for n, (source, target) in enumerate(zip(sources, targets))
    ]
    for copy in copies:
        copy.start()
    return copies


def call(kernel, outs, in_specs, scratch, mib, flops, bytes_moved):
    multiple = isinstance(outs, (list, tuple))
    return pl.pallas_call(
        kernel,
        out_shape=outs,
        in_specs=in_specs,
        out_specs=[VMEM] * len(outs) if multiple else VMEM,
        scratch_shapes=scratch,
        compiler_params=pltpu.CompilerParams(vmem_limit_bytes=mib << 20),
        cost_estimate=pl.CostEstimate(
            flops=flops, bytes_accessed=bytes_moved, transcendentals=0
        ),
    )


def is_odd():
    return lax.axis_index("gy") % 2 == 1


def sublane(shape):
    return lax.broadcasted_iota(jnp.int32, shape, len(shape) - 2)


def pack_kernel(*refs):
    sources, (out_x, out_s), held, sems = refs[:7], refs[7:9], refs[9:16], refs[16]
    sn, sb, rn, rb, sp, an, ti = held
    depth, rows, width = sn.shape
    order = (0, 2, 1, 3, 4, 5, 6)
    copies = fetch([sources[n] for n in order], [held[n] for n in order], sems)
    half = rows // 2
    full = depth * rows
    odd = is_odd()
    for place, field in enumerate((sn, rn)):
        copies[place].wait()
        value = field[...].reshape(full, width).astype(BF16)
        out_x[place * full : (place + 1) * full] = value
        out_s[place * full : (place + 1) * full] = value
    first_half = sublane((depth, rows, width)) < half

    def joined(a, b, start, count):
        keep = first_half[: a.shape[0]]
        turned_a = pltpu.roll(a, half, 1)
        turned_b = pltpu.roll(b, half, 1)
        low = jnp.where(keep, a, turned_b).reshape(count, width).astype(BF16)
        high = jnp.where(keep, turned_a, b).reshape(count, width).astype(BF16)
        out_x[start : start + count] = jnp.where(odd, high, low)
        out_s[start : start + count] = jnp.where(odd, low, high)

    copies[2].wait()
    copies[3].wait()
    joined(sb[...], rb[...], 2 * full, full)
    copies[4].wait()
    copies[5].wait()
    joined(sp[...], an[...], 3 * full, full)
    copies[6].wait()
    joined(ti[: depth // 2], ti[depth // 2 :], 4 * full, full // 2)


def inject_kernel(grid_rows, *refs):
    sources, (inj, bins_y, table), held, (onehot, left, sems) = (
        refs[:6], refs[6:9], refs[9:15], refs[15:],
    )
    rc, rt, sc, sw, bins, weights = held
    copies = fetch(sources, held, sems)
    count = rc.shape[1]
    _, rows, width = bins.shape
    first_row = lax.axis_index("gy") * rows
    half = rows // 2
    shift = width.bit_length() - 1
    power = 1 << shift == width

    def row_of(cell):
        if power:
            return lax.shift_right_logical(cell, jnp.int32(shift))
        return lax.div(cell, jnp.int32(width))

    own = lax.broadcasted_iota(jnp.int32, (rows, 1), 0)
    own_row = first_row + own
    edge = first_row + jnp.where(own < half, own + rows, own - rows)
    edge_row = jnp.where(
        edge >= grid_rows, edge - grid_rows, jnp.where(edge < 0, edge + grid_rows, edge)
    )

    copies[0].wait()
    copies[1].wait()
    for start in range(0, count, LANES):
        cells = rc[:, start : start + LANES]
        at_row = row_of(cells)
        at_col = cells - at_row * width
        cols = lax.broadcasted_iota(jnp.int32, (width, LANES), 0)
        onehot[:, start : start + LANES] = jnp.where(cols == at_col, 1.0, 0.0).astype(BF16)
        parts = []
        for step, wanted in ((0, own_row), (0, edge_row), (1, own_row)):
            amount = rt[step : step + 1, start : start + LANES]
            coarse = amount.astype(BF16).astype(F32)
            fine = amount - coarse
            here = wanted == at_row
            parts.append(jnp.where(here, coarse, 0.0))
            parts.append(jnp.where(here, fine, 0.0))
        left[:, start : start + LANES] = jnp.concatenate(parts, 0).astype(BF16)
    spread = lax.dot_general(
        left[...], onehot[...], (((1,), (1,)), ((), ())), preferred_element_type=F32
    )
    cols = lax.broadcasted_iota(jnp.int32, (rows, width), 1)
    copies[2].wait()
    copies[3].wait()
    for place, (step, wanted) in enumerate(((0, own_row), (0, edge_row), (1, own_row))):
        base = 2 * place * rows
        inj[place, 1] = spread[base : base + rows] + spread[base + rows : base + 2 * rows]
        total = jnp.zeros((rows, width), F32)
        for i in range(sc.shape[0]):
            cell = sc[i]
            at_row = lax.div(cell, jnp.int32(width))
            at_col = cell - at_row * width
            here = jnp.logical_and(wanted == at_row, cols == at_col)
            total = total + jnp.where(here, sw[step, i], 0.0)
        inj[place, 0] = total
    copies[4].wait()
    for y in range(rows):
        bins_y[y] = bins[:, y, :]
    copies[5].wait()
    lag_count, angles, bin_count, lanes = table.shape
    values = weights[...].astype(F32)
    for a in range(angles):
        slab = values[:, a, :]
        for h in range(lag_count):
            table[h, a] = jnp.broadcast_to(slab[:, h : h + 1], (bin_count, lanes))


def shifted_x(value, k, lane):
    width = value.shape[-1]
    above = jnp.where(lane < width - k, pltpu.roll(value, width - k, 1), 0.0)
    below = jnp.where(lane >= k, pltpu.roll(value, k, 1), 0.0)
    return above, below


def flat_terms(value, y_shifts, lane):
    second = (2.0 * SECOND[0]) * value
    first = None
    for k in range(1, REACH + 1):
        above, below = shifted_x(value, k, lane)
        up, down = y_shifts[k - 1]
        second = second + SECOND[k] * ((above + below) + (up + down))
        term = FIRST[k - 1] * ((above - below) + (up - down))
        first = term if first is None else first + term
    return second, first


def depth_terms(field, slope, at):
    second = SECOND[0] * field[at + REACH]
    first = None
    for k in range(1, REACH + 1):
        second = second + SECOND[k] * (field[at + REACH + k] + field[at + REACH - k])
        term = FIRST[k - 1] * (slope[at + REACH + k] - slope[at + REACH - k])
        first = term if first is None else first + term
    return second, first


def step_kernel(
    sn, sb, rn, rb, sp, an, ti, px, ps, inj, out,
    field, slope, base, edge_sp, edge_ti, later, later_edge, turned,
):
    depth, rows, width = sn.shape
    half = rows // 2
    full = depth * rows
    odd = is_odd()
    row = sublane((rows, width))
    lane = lax.broadcasted_iota(jnp.int32, (rows, width), 1)
    low_half = row < half
    now = (sn, rn)
    before = (sb, rb)

    zeros = jnp.zeros((REACH, rows, width), F32)
    for ref in (field, slope):
        for m in range(2):
            for t in range(2):
                ref[m, t, :REACH] = zeros
                ref[m, t, REACH + depth :] = zeros
    for m in range(2):
        later[m, :REACH] = zeros
        later[m, REACH + depth :] = zeros

    def from_packs(start):
        x = px[pl.ds(start, 2 * rows), :].astype(F32)
        s = ps[pl.ds(start, 2 * rows), :].astype(F32)
        return jnp.where(odd, s, x), jnp.where(odd, x, s)

    def roll(value, k):
        return pltpu.roll(value, k % rows, 0)

    def edge_pair(low, high):
        first = jnp.where(low_half, high, roll(low, half))
        second = jnp.where(low_half, roll(high, half), low)
        return first, second

    def tilt_edge(pair, c):
        start = pl.multiple_of(4 * full + pair * 2 * rows, 2 * rows)
        low2, high2 = from_packs(start)
        for j in range(2):
            part = slice(j * rows, (j + 1) * rows)
            a, b = edge_pair(low2[part], high2[part])
            edge_ti[2 * pair + j] = a
            edge_ti[2 * pair + j + depth // 2] = b
        return c

    lax.fori_loop(0, depth // 4, tilt_edge, 0, unroll=2)

    def flat(pair, c):
        offset = pair * 2 * rows
        starts = [pl.multiple_of(n * full + offset, 2 * rows) for n in range(4)]
        current = [from_packs(starts[m]) for m in range(2)]
        old_low, old_high = from_packs(starts[2])
        media_low, media_high = from_packs(starts[3])
        for j in range(2):
            part = slice(j * rows, (j + 1) * rows)
            z = 2 * pair + j
            old = edge_pair(old_low[part], old_high[part])
            speed_edge, aniso_edge = edge_pair(media_low[part], media_high[part])
            edge_sp[z] = speed_edge
            factor = (sp[z] * (1.0 + 2.0 * an[z]), speed_edge * (1.0 + 2.0 * aniso_edge))
            for m in range(2):
                low, high = current[m][0][part], current[m][1][part]
                mid = now[m][z]
                edge = jnp.where(low_half, high, low)
                own_shifts, edge_shifts = [], []
                for k in range(1, REACH + 1):
                    mid_up, mid_down = roll(mid, -k), roll(mid, k)
                    low_up, low_down = roll(low, -k), roll(low, k)
                    high_up, high_down = roll(high, -k), roll(high, k)
                    own_shifts.append(
                        (
                            jnp.where(row < rows - k, mid_up, high_up),
                            jnp.where(row >= k, mid_down, low_down),
                        )
                    )
                    edge_shifts.append(
                        (
                            jnp.where(
                                low_half, high_up, jnp.where(row < rows - k, low_up, mid_up)
                            ),
                            jnp.where(
                                low_half, jnp.where(row >= k, high_down, mid_down), low_down
                            ),
                        )
                    )
                for t, (value, shifts, prior) in enumerate(
                    ((mid, own_shifts, before[m][z]), (edge, edge_shifts, old[m]))
                ):
                    second, first = flat_terms(value, shifts, lane)
                    field[m, t, z + REACH] = value
                    slope[m, t, z + REACH] = first
                    base[m, t, z] = 2.0 * value - prior + factor[t] * second
        return c

    lax.fori_loop(0, depth // 2, flat, 0)

    def deep(z, c):
        speed = (sp[z], edge_sp[z])
        tilt = (ti[z], edge_ti[z])
        for m in range(2):
            for t in range(2):
                second, first = depth_terms(field.at[m, t], slope.at[m, t], z)
                value = base[m, t, z] + speed[t] * (second + tilt[t] * first)
                if t == 0:
                    later[m, z + REACH] = value
                else:
                    later_edge[m, z] = value
        return c

    lax.fori_loop(0, depth, deep, 0, unroll=2)
    for m in range(2):
        later[m, REACH] = later[m, REACH] + inj[0, m]
        later_edge[m, 0] = later_edge[m, 0] + inj[1, m]

    def flat_later(z, c):
        factor = sp[z] * (1.0 + 2.0 * an[z])
        for m in range(2):
            mid = later[m, z + REACH]
            edge = later_edge[m, z]
            shifts = []
            for k in range(1, REACH + 1):
                shifts.append(
                    (
                        jnp.where(row < rows - k, roll(mid, -k), roll(edge, -k)),
                        jnp.where(row >= k, roll(mid, k), roll(edge, k)),
                    )
                )
            second, first = flat_terms(mid, shifts, lane)
            slope[m, 0, z + REACH] = first
            base[m, 0, z] = 2.0 * mid - now[m][z] + factor * second
            for part in range(width // LANES):
                turned[0, m, part, pl.ds(z, rows, stride=depth), :] = mid[
                    :, part * LANES : (part + 1) * LANES
                ]
        return c

    lax.fori_loop(0, depth, flat_later, 0, unroll=2)

    def deep_later(z, c):
        surface = jnp.where(z == 0, 1.0, 0.0)
        for m in range(2):
            second, first = depth_terms(later.at[m], slope.at[m, 0], z)
            value = base[m, 0, z] + sp[z] * (second + ti[z] * first) + surface * inj[2, m]
            for part in range(width // LANES):
                turned[1, m, part, pl.ds(z, rows, stride=depth), :] = value[
                    :, part * LANES : (part + 1) * LANES
                ]
        return c

    lax.fori_loop(0, depth, deep_later, 0, unroll=2)
    for s in range(STEPS):
        for m in range(2):
            for part in range(width // LANES):
                for y in range(rows):
                    out[s, m, y, :, part * LANES : (part + 1) * LANES] = turned[
                        s, m, part, y * depth : (y + 1) * depth, :
                    ].astype(BF16)


def image_kernel(lags_in, far, near, own, chip, relay, bins, table, out, window, turned, lags, sems):
    copies = fetch([lags_in], [lags], sems)
    rows, depth, width = bins.shape
    lag_count, angles = table.shape[:2]
    odd = jnp.where(is_odd(), 1, 0)
    for piece, place in ((far, 0), (near, 1), (own, 2), (chip, 3), (relay, 4)):
        block = (place + odd * (4 - 2 * place)) * rows
        for s in range(STEPS):
            for m in range(2):
                window[s, m, pl.ds(block, rows)] = piece[s, m].astype(F32)
    copies[0].wait()
    tiles = [(z, x) for z in range(0, depth, 8) for x in range(0, width, LANES)]

    def one_row(y, c):
        ids = bins[y]

        def one_lag(h, sums):
            lag = lags[h]
            at_s = y + 2 * rows - lag
            at_r = y + 2 * rows + lag
            sums = [list(a) for a in sums]
            for n, (z, x) in enumerate(tiles):
                zs, xs = slice(z, z + 8), slice(x, x + LANES)
                product = window[0, 0, at_s, zs, xs] * window[0, 1, at_r, zs, xs]
                for s in range(1, STEPS):
                    product = product + window[s, 0, at_s, zs, xs] * window[s, 1, at_r, zs, xs]
                for a in range(angles):
                    weight = jnp.take_along_axis(table[h, a], ids[zs, xs], axis=0)
                    sums[a][n] = sums[a][n] + weight * product
            return tuple(tuple(a) for a in sums)

        zero = jnp.zeros((8, LANES), F32)
        sums = lax.fori_loop(
            0, lag_count, one_lag, tuple((zero,) * len(tiles) for _ in range(angles)), unroll=4
        )
        for a in range(angles):
            for n, (z, x) in enumerate(tiles):
                turned[a, x // LANES, pl.ds(z * rows + y, 8, stride=rows), :] = sums[a][n]
        return c

    lax.fori_loop(0, rows, one_row, 0)
    for a in range(angles):
        for part in range(width // LANES):
            out[a, :, :, part * LANES : (part + 1) * LANES] = (
                turned[a, part].astype(BF16).reshape(depth, rows, LANES)
            )


def per_device(
    source_now, source_before, receiver_now, receiver_before, speed_term, aniso_field,
    tilt_field, angle_bins, weight_table, offset_lags, source_cells, source_wavelet,
    receiver_cells, receiver_traces,
):
    depth, rows, width = source_now.shape
    size = lax.axis_size("gy")
    full = depth * rows
    lag_count, bin_count, angles = weight_table.shape
    count = receiver_cells.shape[0]
    parts = width // LANES

    chip_route = [(i, i ^ 1) for i in range(size)]
    near_route = [(i, (i + 1 if i % 2 else i - 1) % size) for i in range(size)]

    def moved(block, route):
        return lax.ppermute(block, "gy", route)

    fields = (
        source_now, source_before, receiver_now, receiver_before, speed_term, aniso_field,
        tilt_field,
    )
    pack_shape = jax.ShapeDtypeStruct((4 * full + full // 2, width), BF16)
    pack_x, pack_s = call(
        pack_kernel,
        [pack_shape] * 2,
        [HBM] * 7,
        [pltpu.VMEM((depth, rows, width), F32)] * 7 + [pltpu.SemaphoreType.DMA((7,))],
        8,
        full * width * 20,
        full * width * 40,
    )(*in_hbm(fields))
    got_s = moved(pack_s, chip_route)
    got_x = moved(pack_x, near_route)

    inj, bins_y, table = call(
        functools.partial(inject_kernel, size * rows),
        [
            jax.ShapeDtypeStruct((3, 2, rows, width), F32),
            jax.ShapeDtypeStruct((rows, depth, width), jnp.int32),
            jax.ShapeDtypeStruct((lag_count, angles, bin_count, LANES), F32),
        ],
        [HBM] * 6,
        [
            pltpu.VMEM((1, count), jnp.int32),
            pltpu.VMEM((STEPS, count), F32),
            pltpu.SMEM(source_cells.shape, jnp.int32),
            pltpu.SMEM(source_wavelet.shape, F32),
            pltpu.VMEM((depth, rows, width), jnp.int32),
            pltpu.VMEM((bin_count, angles, lag_count), BF16),
            pltpu.VMEM((width, count), BF16),
            pltpu.VMEM((6 * rows, count), BF16),
            pltpu.SemaphoreType.DMA((6,)),
        ],
        8,
        12 * rows * count * width,
        full * width * 8,
    )(
        *in_hbm(
            (
                receiver_cells[None],
                receiver_traces,
                source_cells,
                source_wavelet,
                angle_bins,
                jnp.transpose(weight_table, (1, 2, 0)),
            )
        )
    )

    padded = (2, 2, depth + 2 * REACH, rows, width)
    own = call(
        step_kernel,
        jax.ShapeDtypeStruct((STEPS, 2, rows, depth, width), BF16),
        [VMEM] * 10,
        [
            pltpu.VMEM(padded, F32),
            pltpu.VMEM(padded, F32),
            pltpu.VMEM((2, 2, depth, rows, width), F32),
            pltpu.VMEM((depth, rows, width), F32),
            pltpu.VMEM((depth, rows, width), F32),
            pltpu.VMEM((2, depth + 2 * REACH, rows, width), F32),
            pltpu.VMEM((2, depth, rows, width), F32),
            pltpu.VMEM((STEPS, 2, parts, full, LANES), F32),
        ],
        16,
        full * width * 600,
        full * width * 50,
    )(*fields, got_x, got_s, inj)

    chip = moved(own, chip_route)
    near = moved(own, near_route)
    far = moved(chip, near_route)
    relay = moved(near, chip_route)
    return call(
        image_kernel,
        jax.ShapeDtypeStruct((angles, depth, rows, width), BF16),
        [HBM] + [VMEM] * 7,
        [
            pltpu.VMEM((STEPS, 2, 5 * rows, depth, width), F32),
            pltpu.VMEM((angles, parts, full, LANES), F32),
            pltpu.SMEM(offset_lags.shape, jnp.int32),
            pltpu.SemaphoreType.DMA((1,)),
        ],
        16,
        full * width * 24 * 12,
        full * width * 20,
    )(*in_hbm((offset_lags,)), far, near, own, chip, relay, bins_y, table)


def solution(mesh):
    grid = P("shot", "gy", None)
    media = P(None, "gy", None)
    return jax.shard_map(
        per_device,
        mesh=mesh,
        in_specs=(grid,) * 4
        + (media,) * 4
        + (P(), P(), P("shot"), P("shot", None), P("shot"), P("shot", None)),
        out_specs=P("shot", None, "gy", None),
        check_vma=False,
    )
```

```python
import functools

import jax
import jax.numpy as jnp
from jax import lax
from jax.experimental import pallas as pl
from jax.experimental.pallas import tpu as pltpu
from jax.sharding import PartitionSpec as P


STEPS = 2
SECOND = (-205.0 / 72.0, 8.0 / 5.0, -1.0 / 5.0, 8.0 / 315.0, -1.0 / 560.0)
FIRST = (4.0 / 5.0, -1.0 / 5.0, 4.0 / 105.0, -1.0 / 280.0)
REACH = 4
LANES = 128
F32 = jnp.float32
BF16 = jnp.bfloat16

VMEM = pl.BlockSpec(memory_space=pltpu.VMEM)
HBM = pl.BlockSpec(memory_space=pltpu.HBM)


def in_hbm(arrays):
    return [pltpu.with_memory_space_constraint(array, pltpu.HBM) for array in arrays]


def fetch(sources, targets, sems):
    copies = [
        pltpu.make_async_copy(source, target, sems.at[n])
        for n, (source, target) in enumerate(zip(sources, targets))
    ]
    for copy in copies:
        copy.start()
    return copies


def call(kernel, outs, in_specs, scratch, mib, flops, bytes_moved, place=VMEM):
    multiple = isinstance(outs, (list, tuple))
    return pl.pallas_call(
        kernel,
        out_shape=outs,
        in_specs=in_specs,
        out_specs=[place] * len(outs) if multiple else place,
        scratch_shapes=scratch,
        compiler_params=pltpu.CompilerParams(vmem_limit_bytes=mib << 20),
        cost_estimate=pl.CostEstimate(
            flops=flops, bytes_accessed=bytes_moved, transcendentals=0
        ),
    )


def is_odd():
    return lax.axis_index("gy") % 2 == 1


def sublane(shape):
    return lax.broadcasted_iota(jnp.int32, shape, len(shape) - 2)


def lane_parts(value):
    return [value[:, x : x + LANES] for x in range(0, value.shape[1], LANES)]


def row_roll(value, k):
    return pltpu.roll(value, k % value.shape[0], 0)


def flat_terms(value, edge, row, lane):
    parts = lane_parts(value)
    edges = None if edge is None else lane_parts(edge)
    rows = value.shape[0]
    second = [(2.0 * SECOND[0]) * part for part in parts]
    first = [None] * len(parts)
    for k in range(1, REACH + 1):
        right = [pltpu.roll(part, k, 1) for part in parts]
        left = [pltpu.roll(part, LANES - k, 1) for part in parts]
        for p, part in enumerate(parts):
            below = jnp.where(lane >= k, right[p], right[p - 1] if p else 0.0)
            above = jnp.where(lane < LANES - k, left[p], left[p + 1] if p + 1 < len(parts) else 0.0)
            outer_up = 0.0 if edges is None else row_roll(edges[p], -k)
            outer_down = 0.0 if edges is None else row_roll(edges[p], k)
            up = jnp.where(row < rows - k, row_roll(part, -k), outer_up)
            down = jnp.where(row >= k, row_roll(part, k), outer_down)
            second[p] = second[p] + SECOND[k] * ((above + below) + (up + down))
            term = FIRST[k - 1] * ((above - below) + (up - down))
            first[p] = term if first[p] is None else first[p] + term
    return second, first


def cross_terms(edge, row, sign):
    rows = edge.shape[0]
    second, first = [], []
    for part in lane_parts(edge):
        a = b = None
        for k in range(1, REACH + 1):
            value = jnp.where(
                row < k, row_roll(part, k), jnp.where(row >= rows - k, row_roll(part, -k), 0.0)
            )
            a = SECOND[k] * value if a is None else a + SECOND[k] * value
            b = FIRST[k - 1] * value if b is None else b + FIRST[k - 1] * value
        second.append(a)
        first.append(sign * b)
    return second, first


def depth_second(field, at):
    second = SECOND[0] * field[at + REACH]
    for k in range(1, REACH + 1):
        second = second + SECOND[k] * (field[at + REACH + k] + field[at + REACH - k])
    return second


def depth_first(slope, at):
    first = None
    for k in range(1, REACH + 1):
        term = FIRST[k - 1] * (slope[at + REACH + k] - slope[at + REACH - k])
        first = term if first is None else first + term
    return first


def clear_ends(ref):
    depth = ref.shape[0] - 2 * REACH
    zeros = jnp.zeros((REACH,) + ref.shape[1:], F32)
    ref[:REACH] = zeros
    ref[REACH + depth :] = zeros


def pack_kernel(*refs):
    sources, (out_x, out_s, partial, flat_factor, tilt_factor), rest = refs[:7], refs[7:12], refs[12:]
    (sn, rn, sb, rb, sp, an, ti, slope, base), sems = rest[:9], rest[9]
    depth, rows, width = sp.shape
    half = rows // 2
    full = depth * rows
    odd = is_odd()
    row = sublane((rows, LANES))
    lane = lax.broadcasted_iota(jnp.int32, (rows, LANES), 1)
    order = (0, 2, 1, 3, 4, 5, 6)
    chunk = depth // 2
    inner = pl.ds(REACH, depth)
    targets = (sn.at[inner], rn.at[inner], sb, rb, sp, an, ti)
    copies = []
    for c in range(2):
        span = pl.ds(c * chunk, chunk)
        copies.append(
            fetch(
                [sources[n].at[span] for n in order],
                [target.at[span] for target in targets],
                sems.at[c],
            )
        )
    for ref in (sn, rn):
        clear_ends(ref)
    for m in range(2):
        clear_ends(slope.at[m])

    def flat(z, c):
        factor = sp[z] * (1.0 + 2.0 * an[z])
        flat_factor[z] = factor
        tilt_factor[z] = sp[z] * ti[z]
        for m, (now, before) in enumerate(((sn, sb), (rn, rb))):
            value = now[z + REACH]
            second, first = flat_terms(value, None, row, lane)
            for p in range(width // LANES):
                lanes = slice(p * LANES, (p + 1) * LANES)
                slope[m, z + REACH, :, lanes] = first[p]
                base[m, z, :, lanes] = (
                    2.0 * value[:, lanes] - before[z, :, lanes] + factor[:, lanes] * second[p]
                )
        return c

    for c in range(2):
        for copy in copies[c]:
            copy.wait()
        lax.fori_loop(c * chunk, (c + 1) * chunk, flat, 0, unroll=2)

    def deep(z, c):
        for m, now in enumerate((sn, rn)):
            partial[m, z] = (
                base[m, z]
                + sp[z] * depth_second(now, z)
                + tilt_factor[z] * depth_first(slope.at[m], z)
            )
        return c

    lax.fori_loop(0, depth, deep, 0, unroll=2)
    first_half = sublane((depth, rows, width)) < half

    def joined(a, b, place):
        turned_a = pltpu.roll(a, half, 1)
        turned_b = pltpu.roll(b, half, 1)
        low = jnp.where(first_half, a, turned_b).reshape(full, width).astype(BF16)
        high = jnp.where(first_half, turned_a, b).reshape(full, width).astype(BF16)
        out_x[place * full : (place + 1) * full] = jnp.where(odd, high, low)
        out_s[place * full : (place + 1) * full] = jnp.where(odd, low, high)

    joined(sn[REACH : REACH + depth], rn[REACH : REACH + depth], 0)
    joined(partial[0], partial[1], 1)
    joined(flat_factor[...], tilt_factor[...], 2)


def inject_kernel(grid_rows, *refs):
    sources, now, (inj, bins_y, table, edge_flat, edge_slope), held, (onehot, left, sems) = (
        refs[:6], refs[6:8], refs[8:13], refs[13:19], refs[19:],
    )
    rc, rt, sc, sw, bins, weights = held
    copies = fetch(sources, held, sems)
    count = rc.shape[1]
    depth, rows, width = bins.shape
    first_row = lax.axis_index("gy") * rows
    half = rows // 2
    shift = width.bit_length() - 1
    power = 1 << shift == width

    def row_of(cell):
        if power:
            return lax.shift_right_logical(cell, jnp.int32(shift))
        return lax.div(cell, jnp.int32(width))

    own = lax.broadcasted_iota(jnp.int32, (rows, 1), 0)
    own_row = first_row + own
    edge = first_row + jnp.where(own < half, own + rows, own - rows)
    edge_row = jnp.where(
        edge >= grid_rows, edge - grid_rows, jnp.where(edge < 0, edge + grid_rows, edge)
    )

    copies[0].wait()
    copies[1].wait()
    for start in range(0, count, LANES):
        cells = rc[:, start : start + LANES]
        at_row = row_of(cells)
        at_col = cells - at_row * width
        cols = lax.broadcasted_iota(jnp.int32, (width, LANES), 0)
        onehot[:, start : start + LANES] = jnp.where(cols == at_col, 1.0, 0.0).astype(BF16)
        parts = []
        for step, wanted in ((0, own_row), (0, edge_row), (1, own_row)):
            amount = rt[step : step + 1, start : start + LANES]
            coarse = amount.astype(BF16).astype(F32)
            fine = amount - coarse
            here = wanted == at_row
            parts.append(jnp.where(here, coarse, 0.0))
            parts.append(jnp.where(here, fine, 0.0))
        left[:, start : start + LANES] = jnp.concatenate(parts, 0).astype(BF16)
    spread = lax.dot_general(
        left[...], onehot[...], (((1,), (1,)), ((), ())), preferred_element_type=F32
    )
    cols = lax.broadcasted_iota(jnp.int32, (rows, width), 1)
    copies[2].wait()
    copies[3].wait()
    for place, (step, wanted) in enumerate(((0, own_row), (0, edge_row), (1, own_row))):
        base = 2 * place * rows
        inj[place, 1] = spread[base : base + rows] + spread[base + rows : base + 2 * rows]
        total = jnp.zeros((rows, width), F32)
        for i in range(sc.shape[0]):
            cell = sc[i]
            at_row = lax.div(cell, jnp.int32(width))
            at_col = cell - at_row * width
            here = jnp.logical_and(wanted == at_row, cols == at_col)
            total = total + jnp.where(here, sw[step, i], 0.0)
        inj[place, 0] = total
    copies[4].wait()
    for y in range(rows):
        bins_y[y] = bins[:, y, :]
    copies[5].wait()
    table_rows, angles, bin_count, lanes = table.shape
    lag_count = table_rows - 1
    table[lag_count] = jnp.zeros((angles, bin_count, lanes), F32)
    values = weights[...].astype(F32)
    for a in range(angles):
        slab = values[:, a, :]
        for h in range(lag_count):
            table[h, a] = jnp.broadcast_to(slab[:, h : h + 1], (bin_count, lanes))
    row = sublane((rows, LANES))
    sign = jnp.where(row < half, -1.0, 1.0)
    for m in range(2):
        clear_ends(edge_slope.at[m])

        def edge(z, c, m=m):
            second, first = cross_terms(now[m][z], row, sign)
            for p in range(width // LANES):
                lanes = slice(p * LANES, (p + 1) * LANES)
                edge_flat[m, z, :, lanes] = second[p]
                edge_slope[m, z + REACH, :, lanes] = first[p]
            return c

        lax.fori_loop(0, depth, edge, 0, unroll=2)


def step_kernel(
    sn, rn, sp, partial, flat_factor, tilt_factor, edge_flat, edge_slope, px, ps, inj, out,
    slope, base, edge_base, edge_tilt, later, later_edge, turned,
):
    depth, rows, width = sn.shape
    half = rows // 2
    full = depth * rows
    odd = is_odd()
    row = sublane((rows, LANES))
    lane = lax.broadcasted_iota(jnp.int32, (rows, LANES), 1)
    sign = jnp.where(row < half, -1.0, 1.0)
    low_half = sublane((rows, width)) < half
    now = (sn, rn)
    parts = [slice(x, x + LANES) for x in range(0, width, LANES)]
    for m in range(2):
        clear_ends(slope.at[m])
        clear_ends(later.at[m])

    def from_packs(start):
        x = px[pl.ds(start, 2 * rows), :].astype(F32)
        s = ps[pl.ds(start, 2 * rows), :].astype(F32)
        return jnp.where(odd, s, x), jnp.where(odd, x, s)

    def edge_pair(low, high):
        first = jnp.where(low_half, high, row_roll(low, half))
        second = jnp.where(low_half, row_roll(high, half), low)
        return first, second

    def flat(pair, c):
        got = [
            from_packs(pl.multiple_of(n * full + pair * 2 * rows, 2 * rows)) for n in range(3)
        ]
        for j in range(2):
            part = slice(j * rows, (j + 1) * rows)
            z = 2 * pair + j
            edges, partials, factors = [edge_pair(low[part], high[part]) for low, high in got]
            edge_tilt[z] = factors[1]
            for m in range(2):
                edge_base[m, z] = partials[m] + factors[0] * edge_flat[m, z]
                second, first = cross_terms(edges[m], row, sign)
                for p, lanes in enumerate(parts):
                    slope[m, z + REACH, :, lanes] = first[p]
                    base[m, z, :, lanes] = (
                        partial[m, z, :, lanes] + flat_factor[z, :, lanes] * second[p]
                    )
        return c

    lax.fori_loop(0, depth // 2, flat, 0)

    def deep(z, c):
        for m in range(2):
            later[m, z + REACH] = base[m, z] + tilt_factor[z] * depth_first(slope.at[m], z)
            later_edge[m, z] = edge_base[m, z] + edge_tilt[z] * depth_first(edge_slope.at[m], z)
        return c

    lax.fori_loop(0, depth, deep, 0, unroll=2)
    for m in range(2):
        later[m, REACH] = later[m, REACH] + inj[0, m]
        later_edge[m, 0] = later_edge[m, 0] + inj[1, m]

    def flat_later(z, c):
        for m in range(2):
            mid = later[m, z + REACH]
            second, first = flat_terms(mid, later_edge[m, z], row, lane)
            for p, lanes in enumerate(parts):
                slope[m, z + REACH, :, lanes] = first[p]
                base[m, z, :, lanes] = (
                    2.0 * mid[:, lanes]
                    - now[m][z, :, lanes]
                    + flat_factor[z, :, lanes] * second[p]
                )
                turned[0, m, p, pl.ds(z, rows, stride=depth), :] = mid[:, lanes]
        return c

    lax.fori_loop(0, depth, flat_later, 0, unroll=2)

    def deep_later(z, c):
        surface = jnp.where(z == 0, 1.0, 0.0)
        for m in range(2):
            value = (
                base[m, z]
                + sp[z] * depth_second(later.at[m], z)
                + tilt_factor[z] * depth_first(slope.at[m], z)
                + surface * inj[2, m]
            )
            for p, lanes in enumerate(parts):
                turned[1, m, p, pl.ds(z, rows, stride=depth), :] = value[:, lanes]
        return c

    lax.fori_loop(0, depth, deep_later, 0, unroll=2)
    for s in range(STEPS):
        for m in range(2):
            for p, lanes in enumerate(parts):
                for y in range(rows):
                    out[s, m, y, :, lanes] = turned[
                        s, m, p, y * depth : (y + 1) * depth, :
                    ].astype(BF16)


GROUP = 4


def listed(lags, rows, near, picks):
    count = jnp.int32(0)
    total = lags.shape[0]
    for h in range(total):
        lag = lags[h]
        inside = jnp.logical_and(lag <= rows, lag >= -rows)
        picks[0, count] = lag
        picks[1, count] = h
        count = count + jnp.where(inside == near, 1, 0)
    for n in range(GROUP):
        picks[0, count + n] = 0
        picks[1, count + n] = total
    return count


def add_lags(window, table, ids, picks, groups, y, rows, tiles, sums):
    steps = window.shape[0]
    angles = table.shape[1]
    at = y + rows * 2

    def one_group(group, sums):
        sums = [list(a) for a in sums]
        for member in range(GROUP):
            lag = picks[0, group * GROUP + member]
            h = picks[1, group * GROUP + member]
            for n, (z, x) in enumerate(tiles):
                zs, xs = slice(z, z + 8), slice(x, x + LANES)
                product = None
                for s in range(steps):
                    term = window[s, 0, at - lag, zs, xs] * window[s, 1, at + lag, zs, xs]
                    product = term if product is None else product + term
                for a in range(angles):
                    weight = jnp.take_along_axis(
                        table[h, a], ids[n], axis=0, mode="promise_in_bounds"
                    )
                    sums[a][n] = sums[a][n] + weight * product
        return tuple(tuple(a) for a in sums)

    return lax.fori_loop(0, groups, one_group, sums)


def place_pieces(window, pieces, rows):
    odd = jnp.where(is_odd(), 1, 0)
    for piece, place in pieces:
        block = (place + odd * (4 - 2 * place)) * rows
        for s in range(STEPS):
            for m in range(2):
                window[s, m, pl.ds(block, rows)] = piece[s, m].astype(F32)


def near_image_kernel(
    lags_in, near, own, chip, bins, table, out, far_picks, window, lags, picks, sems
):
    copies = fetch([lags_in], [lags], sems)
    rows, depth, width = bins.shape
    angles = table.shape[1]
    place_pieces(window, ((near, 1), (own, 2), (chip, 3)), rows)
    copies[0].wait()
    count = listed(lags, rows, False, picks)
    row = lax.broadcasted_iota(jnp.int32, far_picks.shape, 0)
    lane = lax.broadcasted_iota(jnp.int32, far_picks.shape, 1)
    held = jnp.where(row == 2, count, 0)
    for n in range(lags.shape[0] + GROUP):
        value = jnp.where(row == 0, picks[0, n], picks[1, n])
        held = jnp.where(jnp.logical_and(lane == n, row < 2), value, held)
    far_picks[...] = held
    count = listed(lags, rows, True, picks)
    groups = lax.div(count + (GROUP - 1), GROUP)
    tiles = [(z, x) for z in range(0, depth, 8) for x in range(0, width, LANES)]
    zero = jnp.zeros((8, LANES), F32)

    def one_row(y, c):
        ids = [bins[y, z : z + 8, x : x + LANES] for z, x in tiles]
        sums = tuple((zero,) * len(tiles) for _ in range(angles))
        sums = add_lags(window, table, ids, picks, groups, y, rows, tiles, sums)
        for a in range(angles):
            for n, (z, x) in enumerate(tiles):
                out[a, y, z : z + 8, x : x + LANES] = sums[a][n]
        return c

    lax.fori_loop(0, rows, one_row, 0)


def far_image_kernel(
    before, picks_in, far, near, own, chip, relay, bins, table, out,
    window, turned, staged, picks, sems,
):
    pick = pltpu.make_async_copy(picks_in, picks, sems.at[0])
    pick.start()
    rows, depth, width = bins.shape
    angles = table.shape[1]
    place_pieces(window, ((far, 0), (near, 1), (own, 2), (chip, 3), (relay, 4)), rows)
    pick.wait()
    groups = lax.div(picks[2, 0] + (GROUP - 1), GROUP)
    sends = []
    for part in range(width // LANES):
        lanes = slice(part * LANES, (part + 1) * LANES)
        tiles = [(z, part * LANES) for z in range(0, depth, 8)]

        def one_row(y, c, tiles=tiles, lanes=lanes):
            ids = [bins[y, z : z + 8, lanes] for z, _ in tiles]
            sums = tuple(
                tuple(before[a, y, z : z + 8, lanes] for z, _ in tiles) for a in range(angles)
            )
            sums = add_lags(window, table, ids, picks, groups, y, rows, tiles, sums)
            for a in range(angles):
                for n, (z, _) in enumerate(tiles):
                    turned[a, pl.ds(z * rows + y, 8, stride=rows), :] = sums[a][n]
            return c

        lax.fori_loop(0, rows, one_row, 0)
        for a in range(angles):
            staged[part, a] = turned[a].astype(BF16).reshape(depth, rows, LANES)
        send = pltpu.make_async_copy(
            staged.at[part], out.at[:, :, :, lanes], sems.at[1 + part]
        )
        send.start()
        sends.append(send)
    for send in sends:
        send.wait()


def per_device(
    source_now, source_before, receiver_now, receiver_before, speed_term, aniso_field,
    tilt_field, angle_bins, weight_table, offset_lags, source_cells, source_wavelet,
    receiver_cells, receiver_traces,
):
    depth, rows, width = source_now.shape
    size = lax.axis_size("gy")
    full = depth * rows
    lag_count, bin_count, angles = weight_table.shape
    count = receiver_cells.shape[0]
    parts = width // LANES

    chip_route = [(i, i ^ 1) for i in range(size)]
    near_route = [(i, (i + 1 if i % 2 else i - 1) % size) for i in range(size)]

    def moved(block, route):
        return lax.ppermute(block, "gy", route)

    fields = (
        source_now, source_before, receiver_now, receiver_before, speed_term, aniso_field,
        tilt_field,
    )
    tall = depth + 2 * REACH
    grid = (depth, rows, width)
    pack_shape = jax.ShapeDtypeStruct((3 * full, width), BF16)
    pack_x, pack_s, partial, flat_factor, tilt_factor = call(
        pack_kernel,
        [
            pack_shape,
            pack_shape,
            jax.ShapeDtypeStruct((2,) + grid, F32),
            jax.ShapeDtypeStruct(grid, F32),
            jax.ShapeDtypeStruct(grid, F32),
        ],
        [HBM] * 7,
        [pltpu.VMEM((tall, rows, width), F32)] * 2
        + [pltpu.VMEM(grid, F32)] * 5
        + [
            pltpu.VMEM((2, tall, rows, width), F32),
            pltpu.VMEM((2,) + grid, F32),
            pltpu.SemaphoreType.DMA((2, 7)),
        ],
        8,
        full * width * 200,
        full * width * 40,
    )(*in_hbm(fields))
    got_s = moved(pack_s, chip_route)
    got_x = moved(pack_x, near_route)

    inj, bins_y, table, edge_flat, edge_slope = call(
        functools.partial(inject_kernel, size * rows),
        [
            jax.ShapeDtypeStruct((3, 2, rows, width), F32),
            jax.ShapeDtypeStruct((rows, depth, width), jnp.int32),
            jax.ShapeDtypeStruct((lag_count + 1, angles, bin_count, LANES), F32),
            jax.ShapeDtypeStruct((2,) + grid, F32),
            jax.ShapeDtypeStruct((2, tall, rows, width), F32),
        ],
        [HBM] * 6 + [VMEM] * 2,
        [
            pltpu.VMEM((1, count), jnp.int32),
            pltpu.VMEM((STEPS, count), F32),
            pltpu.SMEM(source_cells.shape, jnp.int32),
            pltpu.SMEM(source_wavelet.shape, F32),
            pltpu.VMEM((depth, rows, width), jnp.int32),
            pltpu.VMEM((bin_count, angles, lag_count), BF16),
            pltpu.VMEM((width, count), BF16),
            pltpu.VMEM((6 * rows, count), BF16),
            pltpu.SemaphoreType.DMA((6,)),
        ],
        8,
        12 * rows * count * width,
        full * width * 8,
    )(
        *in_hbm(
            (
                receiver_cells[None],
                receiver_traces,
                source_cells,
                source_wavelet,
                angle_bins,
                jnp.transpose(weight_table, (1, 2, 0)),
            )
        ),
        source_now,
        receiver_now,
    )

    own = call(
        step_kernel,
        jax.ShapeDtypeStruct((STEPS, 2, rows, depth, width), BF16),
        [VMEM] * 11,
        [
            pltpu.VMEM((2, tall, rows, width), F32),
            pltpu.VMEM((2,) + grid, F32),
            pltpu.VMEM((2,) + grid, F32),
            pltpu.VMEM(grid, F32),
            pltpu.VMEM((2, tall, rows, width), F32),
            pltpu.VMEM((2,) + grid, F32),
            pltpu.VMEM((STEPS, 2, parts, full, LANES), F32),
        ],
        16,
        full * width * 300,
        full * width * 50,
    )(
        source_now, receiver_now, speed_term, partial, flat_factor, tilt_factor, edge_flat,
        edge_slope, got_x, got_s, inj,
    )

    chip = moved(own, chip_route)
    near = moved(own, near_route)
    far = moved(chip, near_route)
    relay = moved(near, chip_route)
    window = pltpu.VMEM((STEPS, 2, 5 * rows, depth, width), F32)
    pick_space = pltpu.SMEM((8, LANES), jnp.int32)
    half_image, far_picks = call(
        near_image_kernel,
        [
            jax.ShapeDtypeStruct((angles, rows, depth, width), F32),
            jax.ShapeDtypeStruct((8, LANES), jnp.int32),
        ],
        [HBM] + [VMEM] * 5,
        [
            window,
            pltpu.SMEM(offset_lags.shape, jnp.int32),
            pick_space,
            pltpu.SemaphoreType.DMA((1,)),
        ],
        16,
        full * width * lag_count * 6,
        full * width * 20,
    )(*in_hbm((offset_lags,)), near, own, chip, bins_y, table)
    return call(
        far_image_kernel,
        jax.ShapeDtypeStruct((angles, depth, rows, width), BF16),
        [VMEM] * 9,
        [
            window,
            pltpu.VMEM((angles, full, LANES), F32),
            pltpu.VMEM((parts, angles, depth, rows, LANES), BF16),
            pick_space,
            pltpu.SemaphoreType.DMA((1 + parts,)),
        ],
        16,
        full * width * lag_count * 6,
        full * width * 20,
        HBM,
    )(half_image, far_picks, far, near, own, chip, relay, bins_y, table)


def solution(mesh):
    grid = P("shot", "gy", None)
    media = P(None, "gy", None)
    return jax.shard_map(
        per_device,
        mesh=mesh,
        in_specs=(grid,) * 4
        + (media,) * 4
        + (P(), P(), P("shot"), P("shot", None), P("shot"), P("shot", None)),
        out_specs=P("shot", None, "gy", None),
        check_vma=False,
    )
```

```python
import functools

import jax
import jax.numpy as jnp
from jax import lax
from jax.experimental import pallas as pl
from jax.experimental.pallas import tpu as pltpu
from jax.sharding import PartitionSpec as P


STEPS = 2
SECOND = (-205.0 / 72.0, 8.0 / 5.0, -1.0 / 5.0, 8.0 / 315.0, -1.0 / 560.0)
FIRST = (4.0 / 5.0, -1.0 / 5.0, 4.0 / 105.0, -1.0 / 280.0)
REACH = 4
LANES = 128
F32 = jnp.float32
BF16 = jnp.bfloat16

VMEM = pl.BlockSpec(memory_space=pltpu.VMEM)
HBM = pl.BlockSpec(memory_space=pltpu.HBM)


def in_hbm(arrays):
    return [pltpu.with_memory_space_constraint(array, pltpu.HBM) for array in arrays]


def fetch(sources, targets, sems):
    copies = [
        pltpu.make_async_copy(source, target, sems.at[n])
        for n, (source, target) in enumerate(zip(sources, targets))
    ]
    for copy in copies:
        copy.start()
    return copies


def call(kernel, outs, in_specs, scratch, mib, flops, bytes_moved, places=None, aliases=None):
    return pl.pallas_call(
        kernel,
        out_shape=outs,
        in_specs=in_specs,
        out_specs=places or [VMEM] * len(outs),
        input_output_aliases=aliases or {},
        scratch_shapes=scratch,
        compiler_params=pltpu.CompilerParams(vmem_limit_bytes=mib << 20),
        cost_estimate=pl.CostEstimate(
            flops=flops, bytes_accessed=bytes_moved, transcendentals=0
        ),
    )


def is_odd():
    return lax.axis_index("gy") % 2 == 1


def sublane(shape):
    return lax.broadcasted_iota(jnp.int32, shape, len(shape) - 2)


def lane_parts(value):
    return [value[:, x : x + LANES] for x in range(0, value.shape[1], LANES)]


def row_roll(value, k):
    return pltpu.roll(value, k % value.shape[0], 0)


def flat_terms(value, edge, row, lane):
    parts = lane_parts(value)
    edges = None if edge is None else lane_parts(edge)
    rows = value.shape[0]
    second = [(2.0 * SECOND[0]) * part for part in parts]
    first = [None] * len(parts)
    for k in range(1, REACH + 1):
        right = [pltpu.roll(part, k, 1) for part in parts]
        left = [pltpu.roll(part, LANES - k, 1) for part in parts]
        for p, part in enumerate(parts):
            below = jnp.where(lane >= k, right[p], right[p - 1] if p else 0.0)
            above = jnp.where(lane < LANES - k, left[p], left[p + 1] if p + 1 < len(parts) else 0.0)
            outer_up = 0.0 if edges is None else row_roll(edges[p], -k)
            outer_down = 0.0 if edges is None else row_roll(edges[p], k)
            up = jnp.where(row < rows - k, row_roll(part, -k), outer_up)
            down = jnp.where(row >= k, row_roll(part, k), outer_down)
            second[p] = second[p] + SECOND[k] * ((above + below) + (up + down))
            term = FIRST[k - 1] * ((above - below) + (up - down))
            first[p] = term if first[p] is None else first[p] + term
    return second, first


def cross_terms(edge, row, sign):
    rows = edge.shape[0]
    second, first = [], []
    for part in lane_parts(edge):
        a = b = None
        for k in range(1, REACH + 1):
            value = jnp.where(
                row < k, row_roll(part, k), jnp.where(row >= rows - k, row_roll(part, -k), 0.0)
            )
            a = SECOND[k] * value if a is None else a + SECOND[k] * value
            b = FIRST[k - 1] * value if b is None else b + FIRST[k - 1] * value
        second.append(a)
        first.append(sign * b)
    return second, first


def depth_second(field, at):
    second = SECOND[0] * field[at + REACH]
    for k in range(1, REACH + 1):
        second = second + SECOND[k] * (field[at + REACH + k] + field[at + REACH - k])
    return second


def depth_first(slope, at):
    first = None
    for k in range(1, REACH + 1):
        term = FIRST[k - 1] * (slope[at + REACH + k] - slope[at + REACH - k])
        first = term if first is None else first + term
    return first


def clear_ends(ref):
    depth = ref.shape[0] - 2 * REACH
    zeros = jnp.zeros((REACH,) + ref.shape[1:], F32)
    ref[:REACH] = zeros
    ref[REACH + depth :] = zeros


def pack_kernel(*refs):
    sources, (out_x, out_s, now, sp, partial, flat_factor, tilt_factor), rest = (
        refs[:7], refs[7:14], refs[14:],
    )
    (sb, rb, an, ti, slope, base), sems = rest[:6], rest[6]
    sn, rn = now.at[0], now.at[1]
    depth, rows, width = sp.shape
    half = rows // 2
    full = depth * rows
    odd = is_odd()
    row = sublane((rows, LANES))
    lane = lax.broadcasted_iota(jnp.int32, (rows, LANES), 1)
    order = (0, 2, 1, 3, 4, 5, 6)
    chunks = 4
    chunk = depth // chunks
    inner = pl.ds(REACH, depth)
    targets = (sn.at[inner], rn.at[inner], sb, rb, sp, an, ti)
    copies = []
    for c in range(chunks):
        span = pl.ds(c * chunk, chunk)
        copies.append(
            fetch(
                [sources[n].at[span] for n in order],
                [target.at[span] for target in targets],
                sems.at[c],
            )
        )
    for ref in (sn, rn):
        clear_ends(ref)
    for m in range(2):
        clear_ends(slope.at[m])

    def flat(z, c):
        factor = sp[z] * (1.0 + 2.0 * an[z])
        flat_factor[z] = factor
        tilt_factor[z] = sp[z] * ti[z]
        for m, before in enumerate((sb, rb)):
            value = now[m, z + REACH]
            second, first = flat_terms(value, None, row, lane)
            for p in range(width // LANES):
                lanes = slice(p * LANES, (p + 1) * LANES)
                slope[m, z + REACH, :, lanes] = first[p]
                base[m, z, :, lanes] = (
                    2.0 * value[:, lanes] - before[z, :, lanes] + factor[:, lanes] * second[p]
                )
        return c

    def deep(z, c):
        for m in range(2):
            partial[m, z] = (
                base[m, z]
                + sp[z] * depth_second(now.at[m], z)
                + tilt_factor[z] * depth_first(slope.at[m], z)
            )
        return c

    for c in range(chunks):
        for copy in copies[c]:
            copy.wait()
        lax.fori_loop(c * chunk, (c + 1) * chunk, flat, 0, unroll=4)
        done = (c + 1) * chunk if c == chunks - 1 else max((c + 1) * chunk - REACH, 0)
        start = max(c * chunk - REACH, 0)
        if done > start:
            lax.fori_loop(start, done, deep, 0, unroll=4)
    first_half = sublane((depth, rows, width)) < half

    def joined(a, b, place):
        turned_a = pltpu.roll(a, half, 1)
        turned_b = pltpu.roll(b, half, 1)
        low = jnp.where(first_half, a, turned_b).reshape(full, width).astype(BF16)
        high = jnp.where(first_half, turned_a, b).reshape(full, width).astype(BF16)
        out_x[place * full : (place + 1) * full] = jnp.where(odd, high, low)
        out_s[place * full : (place + 1) * full] = jnp.where(odd, low, high)

    joined(now[0, REACH : REACH + depth], now[1, REACH : REACH + depth], 0)
    joined(partial[0], partial[1], 1)
    joined(flat_factor[...], tilt_factor[...], 2)


def inject_kernel(grid_rows, *refs):
    sources, now, (inj, bins_y, table, edge_flat, edge_slope), held, (onehot, left, sems) = (
        refs[:6], refs[6], refs[7:12], refs[12:18], refs[18:],
    )
    rc, rt, sc, sw, bins, weights = held
    copies = fetch(sources, held, sems)
    count = rc.shape[1]
    depth, rows, width = bins.shape
    first_row = lax.axis_index("gy") * rows
    half = rows // 2
    shift = width.bit_length() - 1
    power = 1 << shift == width

    def row_of(cell):
        if power:
            return lax.shift_right_logical(cell, jnp.int32(shift))
        return lax.div(cell, jnp.int32(width))

    own = lax.broadcasted_iota(jnp.int32, (rows, 1), 0)
    own_row = first_row + own
    edge = first_row + jnp.where(own < half, own + rows, own - rows)
    edge_row = jnp.where(
        edge >= grid_rows, edge - grid_rows, jnp.where(edge < 0, edge + grid_rows, edge)
    )

    copies[0].wait()
    copies[1].wait()
    for start in range(0, count, LANES):
        cells = rc[:, start : start + LANES]
        at_row = row_of(cells)
        at_col = cells - at_row * width
        cols = lax.broadcasted_iota(jnp.int32, (width, LANES), 0)
        onehot[:, start : start + LANES] = jnp.where(cols == at_col, 1.0, 0.0).astype(BF16)
        parts = []
        for step, wanted in ((0, own_row), (0, edge_row), (1, own_row)):
            amount = rt[step : step + 1, start : start + LANES]
            coarse = amount.astype(BF16).astype(F32)
            fine = amount - coarse
            here = wanted == at_row
            parts.append(jnp.where(here, coarse, 0.0))
            parts.append(jnp.where(here, fine, 0.0))
        left[:, start : start + LANES] = jnp.concatenate(parts, 0).astype(BF16)
    spread = lax.dot_general(
        left[...], onehot[...], (((1,), (1,)), ((), ())), preferred_element_type=F32
    )
    cols = lax.broadcasted_iota(jnp.int32, (rows, width), 1)
    copies[2].wait()
    copies[3].wait()
    for place, (step, wanted) in enumerate(((0, own_row), (0, edge_row), (1, own_row))):
        base = 2 * place * rows
        inj[place, 1] = spread[base : base + rows] + spread[base + rows : base + 2 * rows]
        total = jnp.zeros((rows, width), F32)
        for i in range(sc.shape[0]):
            cell = sc[i]
            at_row = lax.div(cell, jnp.int32(width))
            at_col = cell - at_row * width
            here = jnp.logical_and(wanted == at_row, cols == at_col)
            total = total + jnp.where(here, sw[step, i], 0.0)
        inj[place, 0] = total
    copies[4].wait()
    for y in range(rows):
        bins_y[y] = bins[:, y, :]
    copies[5].wait()
    table_rows, angles, bin_count, lanes = table.shape
    lag_count = table_rows - 1
    table[lag_count] = jnp.zeros((angles, bin_count, lanes), F32)
    values = weights[...].astype(F32)
    for a in range(angles):
        slab = values[:, a, :]
        for h in range(lag_count):
            table[h, a] = jnp.broadcast_to(slab[:, h : h + 1], (bin_count, lanes))
    row = sublane((rows, LANES))
    sign = jnp.where(row < half, -1.0, 1.0)
    for m in range(2):
        clear_ends(edge_slope.at[m])

        def edge(z, c, m=m):
            second, first = cross_terms(now[m, z + REACH], row, sign)
            for p in range(width // LANES):
                lanes = slice(p * LANES, (p + 1) * LANES)
                edge_flat[m, z, :, lanes] = second[p]
                edge_slope[m, z + REACH, :, lanes] = first[p]
            return c

        lax.fori_loop(0, depth, edge, 0, unroll=2)


def step_kernel(
    now, sp, partial, flat_factor, tilt_factor, edge_flat, edge_slope, px, ps, inj,
    out, slim, known,
    slope, base, edge_base, edge_tilt, later, later_edge, turned,
):
    depth, rows, width = sp.shape
    half = rows // 2
    full = depth * rows
    odd = is_odd()
    row = sublane((rows, LANES))
    lane = lax.broadcasted_iota(jnp.int32, (rows, LANES), 1)
    sign = jnp.where(row < half, -1.0, 1.0)
    low_half = sublane((rows, width)) < half
    parts = [slice(x, x + LANES) for x in range(0, width, LANES)]
    for m in range(2):
        clear_ends(slope.at[m])
        clear_ends(later.at[m])

    def from_packs(start):
        x = px[pl.ds(start, 2 * rows), :].astype(F32)
        s = ps[pl.ds(start, 2 * rows), :].astype(F32)
        return jnp.where(odd, s, x), jnp.where(odd, x, s)

    def edge_pair(low, high):
        first = jnp.where(low_half, high, row_roll(low, half))
        second = jnp.where(low_half, row_roll(high, half), low)
        return first, second

    def flat(pair, c):
        got = [
            from_packs(pl.multiple_of(n * full + pair * 2 * rows, 2 * rows)) for n in range(3)
        ]
        for j in range(2):
            part = slice(j * rows, (j + 1) * rows)
            z = 2 * pair + j
            edges, partials, factors = [edge_pair(low[part], high[part]) for low, high in got]
            edge_tilt[z] = factors[1]
            for m in range(2):
                edge_base[m, z] = partials[m] + factors[0] * edge_flat[m, z]
                second, first = cross_terms(edges[m], row, sign)
                for p, lanes in enumerate(parts):
                    slope[m, z + REACH, :, lanes] = first[p]
                    base[m, z, :, lanes] = (
                        partial[m, z, :, lanes] + flat_factor[z, :, lanes] * second[p]
                    )
        return c

    lax.fori_loop(0, depth // 2, flat, 0, unroll=2)

    def deep(z, c):
        for m in range(2):
            later[m, z + REACH] = base[m, z] + tilt_factor[z] * depth_first(slope.at[m], z)
            later_edge[m, z] = edge_base[m, z] + edge_tilt[z] * depth_first(edge_slope.at[m], z)
        return c

    lax.fori_loop(0, depth, deep, 0, unroll=4)
    for m in range(2):
        later[m, REACH] = later[m, REACH] + inj[0, m]
        later_edge[m, 0] = later_edge[m, 0] + inj[1, m]

    def flat_later(z, c):
        for m in range(2):
            mid = later[m, z + REACH]
            second, first = flat_terms(mid, later_edge[m, z], row, lane)
            for p, lanes in enumerate(parts):
                slope[m, z + REACH, :, lanes] = first[p]
                base[m, z, :, lanes] = (
                    2.0 * mid[:, lanes]
                    - now[m, z + REACH, :, lanes]
                    + flat_factor[z, :, lanes] * second[p]
                )
                turned[0, m, p, pl.ds(z, rows, stride=depth), :] = mid[:, lanes]
                turned[2, m, p, pl.ds(z, rows, stride=depth), :] = later_edge[m, z, :, lanes]
        return c

    lax.fori_loop(0, depth, flat_later, 0, unroll=4)

    def deep_later(z, c):
        surface = jnp.where(z == 0, 1.0, 0.0)
        for m in range(2):
            value = (
                base[m, z]
                + sp[z] * depth_second(later.at[m], z)
                + tilt_factor[z] * depth_first(slope.at[m], z)
                + surface * inj[2, m]
            )
            for p, lanes in enumerate(parts):
                turned[1, m, p, pl.ds(z, rows, stride=depth), :] = value[:, lanes]
        return c

    lax.fori_loop(0, depth, deep_later, 0, unroll=4)
    kept = jnp.where(odd, 0, half)
    for m in range(2):
        for p, lanes in enumerate(parts):
            for y in range(rows):
                plane = slice(y * depth, (y + 1) * depth)
                out[0, m, y, :, lanes] = turned[0, m, p, plane, :].astype(BF16)
                last = turned[1, m, p, plane, :].astype(BF16)
                out[1, m, y, :, lanes] = last
                slim[(m + 1) * rows + y, :, lanes] = last
            for y in range(half):
                plane = pl.ds(pl.multiple_of((kept + y) * depth, depth), depth)
                slim[m * half + y, :, lanes] = turned[0, m, p, plane, :].astype(BF16)
                known[m, y, :, lanes] = turned[2, m, p, plane, :].astype(BF16)


GROUP = 4


def listed(lags, rows, near, picks):
    count = jnp.int32(0)
    total = lags.shape[0]
    for h in range(total):
        lag = lags[h]
        inside = jnp.logical_and(lag <= rows, lag >= -rows)
        picks[0, count] = lag
        picks[1, count] = h
        count = count + jnp.where(inside == near, 1, 0)
    for n in range(GROUP):
        picks[0, count + n] = 0
        picks[1, count + n] = total
    return count


PAIR = 2


def add_lags(window, table, ids, picks, groups, rows, spots, sums):
    steps = window.shape[0]
    angles = table.shape[1]

    def one_group(group, sums):
        sums = [list(a) for a in sums]
        for member in range(GROUP):
            lag = picks[0, group * GROUP + member]
            h = picks[1, group * GROUP + member]
            for n, (y, z, x) in enumerate(spots):
                at = y + 2 * rows
                zs, xs = slice(z, z + 8), slice(x, x + LANES)
                product = None
                for s in range(steps):
                    term = window[s, 0, at - lag, zs, xs] * window[s, 1, at + lag, zs, xs]
                    product = term if product is None else product + term
                for a in range(angles):
                    weight = jnp.take_along_axis(
                        table[h, a], ids[n], axis=0, mode="promise_in_bounds"
                    )
                    sums[a][n] = sums[a][n] + weight * product
        return tuple(tuple(a) for a in sums)

    return lax.fori_loop(0, groups, one_group, sums)


def block_of(place):
    return place + jnp.where(is_odd(), 4 - 2 * place, 0)


def place_whole(window, piece, place, rows):
    for s in range(STEPS):
        for m in range(2):
            window[s, m, pl.ds(block_of(place) * rows, rows)] = piece[s, m].astype(F32)


def place_slim(window, slim, known, place, kept, rows):
    half = rows // 2
    start = block_of(place) * rows
    for m in range(2):
        window[0, m, pl.ds(start + kept, half)] = known[m].astype(F32)
        window[0, m, pl.ds(start + half - kept, half)] = slim[
            m * half : (m + 1) * half
        ].astype(F32)
        window[1, m, pl.ds(start, rows)] = slim[(m + 1) * rows : (m + 2) * rows].astype(F32)


def near_image_kernel(
    lags_in, near, known, own, chip, bins, table, out, far_picks, window, lags, picks, sems
):
    copies = fetch([lags_in], [lags], sems)
    rows, depth, width = bins.shape
    angles = table.shape[1]
    kept = jnp.where(is_odd(), 0, rows // 2)
    place_slim(window, near, known, 1, kept, rows)
    place_whole(window, own, 2, rows)
    place_whole(window, chip, 3, rows)
    copies[0].wait()
    count = listed(lags, rows, False, picks)
    row = lax.broadcasted_iota(jnp.int32, far_picks.shape, 0)
    lane = lax.broadcasted_iota(jnp.int32, far_picks.shape, 1)
    held = jnp.where(row == 2, count, 0)
    for n in range(lags.shape[0] + GROUP):
        value = jnp.where(row == 0, picks[0, n], picks[1, n])
        held = jnp.where(jnp.logical_and(lane == n, row < 2), value, held)
    far_picks[...] = held
    count = listed(lags, rows, True, picks)
    groups = lax.div(count + (GROUP - 1), GROUP)
    tiles = [(z, x) for z in range(0, depth, 8) for x in range(0, width, LANES)]
    zero = jnp.zeros((8, LANES), F32)

    def one_row(y, c):
        ids = [bins[y, z : z + 8, x : x + LANES] for z, x in tiles]
        spots = [(y, z, x) for z, x in tiles]
        sums = tuple((zero,) * len(tiles) for _ in range(angles))
        sums = add_lags(window, table, ids, picks, groups, rows, spots, sums)
        for a in range(angles):
            for n, (z, x) in enumerate(tiles):
                out[a, y, z : z + 8, x : x + LANES] = sums[a][n]
        return c

    lax.fori_loop(0, rows, one_row, 0)


def far_image_kernel(
    before, picks_in, window_in, far, relay, hint, bins, table, out, window,
    turned, staged, picks, sems,
):
    del window_in
    rows, depth, width = bins.shape
    angles = table.shape[1]
    half = rows // 2
    for n in range(table.shape[0] - 1 + GROUP):
        picks[0, n] = picks_in[0, n]
        picks[1, n] = picks_in[1, n]
    groups = lax.div(picks_in[2, 0] + (GROUP - 1), GROUP)
    place_whole(window, far, 0, rows)
    place_slim(window, relay, hint, 4, jnp.where(is_odd(), half, 0), rows)
    sends = []
    for piece in range(depth // 8):
        zs = slice(piece * 8, (piece + 1) * 8)
        tiles = [(piece * 8, x) for x in range(0, width, LANES)]

        def some_rows(pair, c, tiles=tiles):
            spots = [(PAIR * pair + r, z, x) for r in range(PAIR) for z, x in tiles]
            ids = [bins[y, z : z + 8, x : x + LANES] for y, z, x in spots]
            sums = tuple(
                tuple(before[a, y, z : z + 8, x : x + LANES] for y, z, x in spots)
                for a in range(angles)
            )
            sums = add_lags(window, table, ids, picks, groups, rows, spots, sums)
            for a in range(angles):
                for n, (y, z, x) in enumerate(spots):
                    turned[a, x // LANES, pl.ds(y, 8, stride=rows), :] = sums[a][n]
            return c

        lax.fori_loop(0, rows // PAIR, some_rows, 0)
        for a in range(angles):
            for n, (_, x) in enumerate(tiles):
                staged[piece, a, :, :, x : x + LANES] = (
                    turned[a, n].astype(BF16).reshape(8, rows, LANES)
                )
        send = pltpu.make_async_copy(staged.at[piece], out.at[:, zs], sems.at[1 + piece])
        send.start()
        sends.append(send)
    for send in sends:
        send.wait()


def per_device(
    source_now, source_before, receiver_now, receiver_before, speed_term, aniso_field,
    tilt_field, angle_bins, weight_table, offset_lags, source_cells, source_wavelet,
    receiver_cells, receiver_traces,
):
    depth, rows, width = source_now.shape
    size = lax.axis_size("gy")
    full = depth * rows
    lag_count, bin_count, angles = weight_table.shape
    count = receiver_cells.shape[0]
    parts = width // LANES

    chip_route = [(i, i ^ 1) for i in range(size)]
    near_route = [(i, (i + 1 if i % 2 else i - 1) % size) for i in range(size)]

    def moved(block, route):
        return lax.ppermute(block, "gy", route)

    fields = (
        source_now, source_before, receiver_now, receiver_before, speed_term, aniso_field,
        tilt_field,
    )
    tall = depth + 2 * REACH
    grid = (depth, rows, width)
    pack_shape = jax.ShapeDtypeStruct((3 * full, width), BF16)
    pack_x, pack_s, now, speed, partial, flat_factor, tilt_factor = call(
        pack_kernel,
        [
            pack_shape,
            pack_shape,
            jax.ShapeDtypeStruct((2, tall, rows, width), F32),
            jax.ShapeDtypeStruct(grid, F32),
            jax.ShapeDtypeStruct((2,) + grid, F32),
            jax.ShapeDtypeStruct(grid, F32),
            jax.ShapeDtypeStruct(grid, F32),
        ],
        [HBM] * 7,
        [pltpu.VMEM(grid, F32)] * 4
        + [
            pltpu.VMEM((2, tall, rows, width), F32),
            pltpu.VMEM((2,) + grid, F32),
            pltpu.SemaphoreType.DMA((4, 7)),
        ],
        8,
        full * width * 200,
        full * width * 40,
    )(*in_hbm(fields))
    got_s = moved(pack_s, chip_route)
    got_x = moved(pack_x, near_route)

    inj, bins_y, table, edge_flat, edge_slope = call(
        functools.partial(inject_kernel, size * rows),
        [
            jax.ShapeDtypeStruct((3, 2, rows, width), F32),
            jax.ShapeDtypeStruct((rows, depth, width), jnp.int32),
            jax.ShapeDtypeStruct((lag_count + 1, angles, bin_count, LANES), F32),
            jax.ShapeDtypeStruct((2,) + grid, F32),
            jax.ShapeDtypeStruct((2, tall, rows, width), F32),
        ],
        [HBM] * 6 + [VMEM],
        [
            pltpu.VMEM((1, count), jnp.int32),
            pltpu.VMEM((STEPS, count), F32),
            pltpu.SMEM(source_cells.shape, jnp.int32),
            pltpu.SMEM(source_wavelet.shape, F32),
            pltpu.VMEM((depth, rows, width), jnp.int32),
            pltpu.VMEM((bin_count, angles, lag_count), BF16),
            pltpu.VMEM((width, count), BF16),
            pltpu.VMEM((6 * rows, count), BF16),
            pltpu.SemaphoreType.DMA((6,)),
        ],
        8,
        12 * rows * count * width,
        full * width * 8,
    )(
        *in_hbm(
            (
                receiver_cells[None],
                receiver_traces,
                source_cells,
                source_wavelet,
                angle_bins,
                jnp.transpose(weight_table, (1, 2, 0)),
            )
        ),
        now,
    )

    half = rows // 2
    own, slim, known = call(
        step_kernel,
        [
            jax.ShapeDtypeStruct((STEPS, 2, rows, depth, width), BF16),
            jax.ShapeDtypeStruct((2 * (half + rows), depth, width), BF16),
            jax.ShapeDtypeStruct((2, half, depth, width), BF16),
        ],
        [VMEM] * 10,
        [
            pltpu.VMEM((2, tall, rows, width), F32),
            pltpu.VMEM((2,) + grid, F32),
            pltpu.VMEM((2,) + grid, F32),
            pltpu.VMEM(grid, F32),
            pltpu.VMEM((2, tall, rows, width), F32),
            pltpu.VMEM((2,) + grid, F32),
            pltpu.VMEM((STEPS + 1, 2, parts, full, LANES), F32),
        ],
        16,
        full * width * 300,
        full * width * 50,
    )(
        now, speed, partial, flat_factor, tilt_factor, edge_flat, edge_slope, got_x, got_s, inj,
    )

    chip = moved(own, chip_route)
    near = moved(slim, near_route)
    far = moved(chip, near_route)
    hint = moved(known, chip_route)
    relay = moved(near, chip_route)
    window_shape = jax.ShapeDtypeStruct((STEPS, 2, 5 * rows, depth, width), F32)
    pick_space = pltpu.SMEM((8, LANES), jnp.int32)
    half_image, far_picks, window = call(
        near_image_kernel,
        [
            jax.ShapeDtypeStruct((angles, rows, depth, width), F32),
            jax.ShapeDtypeStruct((8, LANES), jnp.int32),
            window_shape,
        ],
        [HBM] + [VMEM] * 6,
        [
            pltpu.SMEM(offset_lags.shape, jnp.int32),
            pick_space,
            pltpu.SemaphoreType.DMA((1,)),
        ],
        16,
        full * width * lag_count * 6,
        full * width * 20,
    )(*in_hbm((offset_lags,)), near, known, own, chip, bins_y, table)
    pieces = depth // 8
    return call(
        far_image_kernel,
        [jax.ShapeDtypeStruct((angles, depth, rows, width), BF16), window_shape],
        [VMEM] * 8,
        [
            pltpu.VMEM((angles, parts, 8 * rows, LANES), F32),
            pltpu.VMEM((pieces, angles, 8, rows, width), BF16),
            pick_space,
            pltpu.SemaphoreType.DMA((1 + pieces,)),
        ],
        16,
        full * width * lag_count * 6,
        full * width * 20,
        [HBM, VMEM],
        {2: 1},
    )(half_image, far_picks, window, far, relay, hint, bins_y, table)[0]


def solution(mesh):
    grid = P("shot", "gy", None)
    media = P(None, "gy", None)
    return jax.shard_map(
        per_device,
        mesh=mesh,
        in_specs=(grid,) * 4
        + (media,) * 4
        + (P(), P(), P("shot"), P("shot", None), P("shot"), P("shot", None)),
        out_specs=P("shot", None, "gy", None),
        check_vma=False,
    )
```

```python
import functools

import jax
import jax.numpy as jnp
from jax import lax
from jax.experimental import pallas as pl
from jax.experimental.pallas import tpu as pltpu
from jax.sharding import PartitionSpec as P


STEPS = 2
SECOND = (-205.0 / 72.0, 8.0 / 5.0, -1.0 / 5.0, 8.0 / 315.0, -1.0 / 560.0)
FIRST = (4.0 / 5.0, -1.0 / 5.0, 4.0 / 105.0, -1.0 / 280.0)
REACH = 4
LANES = 128
F32 = jnp.float32
BF16 = jnp.bfloat16

VMEM = pl.BlockSpec(memory_space=pltpu.VMEM)
HBM = pl.BlockSpec(memory_space=pltpu.HBM)


def in_hbm(arrays):
    return [pltpu.with_memory_space_constraint(array, pltpu.HBM) for array in arrays]


def fetch(sources, targets, sems):
    copies = [
        pltpu.make_async_copy(source, target, sems.at[n])
        for n, (source, target) in enumerate(zip(sources, targets))
    ]
    for copy in copies:
        copy.start()
    return copies


def call(kernel, outs, in_specs, scratch, mib, flops, bytes_moved, places=None, aliases=None):
    return pl.pallas_call(
        kernel,
        out_shape=outs,
        in_specs=in_specs,
        out_specs=places or [VMEM] * len(outs),
        input_output_aliases=aliases or {},
        scratch_shapes=scratch,
        compiler_params=pltpu.CompilerParams(vmem_limit_bytes=mib << 20),
        cost_estimate=pl.CostEstimate(
            flops=flops, bytes_accessed=bytes_moved, transcendentals=0
        ),
    )


def is_odd():
    return lax.axis_index("gy") % 2 == 1


def sublane(shape):
    return lax.broadcasted_iota(jnp.int32, shape, len(shape) - 2)


def lane_parts(value):
    return [value[:, x : x + LANES] for x in range(0, value.shape[1], LANES)]


def row_roll(value, k):
    return pltpu.roll(value, k % value.shape[0], 0)


def flat_terms(value, edge, row, lane):
    parts = lane_parts(value)
    edges = None if edge is None else lane_parts(edge)
    rows = value.shape[0]
    second = [(2.0 * SECOND[0]) * part for part in parts]
    first = [None] * len(parts)
    for k in range(1, REACH + 1):
        right = [pltpu.roll(part, k, 1) for part in parts]
        left = [pltpu.roll(part, LANES - k, 1) for part in parts]
        for p, part in enumerate(parts):
            below = jnp.where(lane >= k, right[p], right[p - 1] if p else 0.0)
            above = jnp.where(lane < LANES - k, left[p], left[p + 1] if p + 1 < len(parts) else 0.0)
            outer_up = 0.0 if edges is None else row_roll(edges[p], -k)
            outer_down = 0.0 if edges is None else row_roll(edges[p], k)
            up = jnp.where(row < rows - k, row_roll(part, -k), outer_up)
            down = jnp.where(row >= k, row_roll(part, k), outer_down)
            ahead, behind = above + up, below + down
            second[p] = second[p] + SECOND[k] * (ahead + behind)
            term = FIRST[k - 1] * (ahead - behind)
            first[p] = term if first[p] is None else first[p] + term
    return second, first


def cross_terms(edge, row, sign):
    rows = edge.shape[0]
    second, first = [], []
    for part in lane_parts(edge):
        a = b = None
        for k in range(1, REACH + 1):
            value = jnp.where(
                row < k, row_roll(part, k), jnp.where(row >= rows - k, row_roll(part, -k), 0.0)
            )
            a = SECOND[k] * value if a is None else a + SECOND[k] * value
            b = FIRST[k - 1] * value if b is None else b + FIRST[k - 1] * value
        second.append(a)
        first.append(sign * b)
    return second, first


def depth_second(field, at):
    second = SECOND[0] * field[at + REACH]
    for k in range(1, REACH + 1):
        second = second + SECOND[k] * (field[at + REACH + k] + field[at + REACH - k])
    return second


def depth_first(slope, at):
    first = None
    for k in range(1, REACH + 1):
        term = FIRST[k - 1] * (slope[at + REACH + k] - slope[at + REACH - k])
        first = term if first is None else first + term
    return first


def clear_ends(ref):
    depth = ref.shape[0] - 2 * REACH
    zeros = jnp.zeros((REACH,) + ref.shape[1:], F32)
    ref[:REACH] = zeros
    ref[REACH + depth :] = zeros


def pack_kernel(*refs):
    sources, (out_x, out_s, now, sp, partial, flat_factor, tilt_factor), rest = (
        refs[:7], refs[7:14], refs[14:],
    )
    (sb, rb, an, ti, slope, base), sems = rest[:6], rest[6]
    sn, rn = now.at[0], now.at[1]
    depth, rows, width = sp.shape
    half = rows // 2
    full = depth * rows
    odd = is_odd()
    row = sublane((rows, LANES))
    lane = lax.broadcasted_iota(jnp.int32, (rows, LANES), 1)
    order = (0, 2, 1, 3, 4, 5, 6)
    chunks = 4
    chunk = depth // chunks
    inner = pl.ds(REACH, depth)
    targets = (sn.at[inner], rn.at[inner], sb, rb, sp, an, ti)
    copies = []
    for c in range(chunks):
        span = pl.ds(c * chunk, chunk)
        copies.append(
            fetch(
                [sources[n].at[span] for n in order],
                [target.at[span] for target in targets],
                sems.at[c],
            )
        )
    for ref in (sn, rn):
        clear_ends(ref)
    for m in range(2):
        clear_ends(slope.at[m])

    def flat(z, c):
        factor = sp[z] * (1.0 + 2.0 * an[z])
        flat_factor[z] = factor
        tilt_factor[z] = sp[z] * ti[z]
        for m, before in enumerate((sb, rb)):
            value = now[m, z + REACH]
            second, first = flat_terms(value, None, row, lane)
            for p in range(width // LANES):
                lanes = slice(p * LANES, (p + 1) * LANES)
                slope[m, z + REACH, :, lanes] = first[p]
                base[m, z, :, lanes] = (
                    2.0 * value[:, lanes] - before[z, :, lanes] + factor[:, lanes] * second[p]
                )
        return c

    def deep(z, c):
        for m in range(2):
            partial[m, z] = (
                base[m, z]
                + sp[z] * depth_second(now.at[m], z)
                + tilt_factor[z] * depth_first(slope.at[m], z)
            )
        return c

    for c in range(chunks):
        for copy in copies[c]:
            copy.wait()
        lax.fori_loop(c * chunk, (c + 1) * chunk, flat, 0, unroll=4)
        done = (c + 1) * chunk if c == chunks - 1 else max((c + 1) * chunk - REACH, 0)
        start = max(c * chunk - REACH, 0)
        if done > start:
            lax.fori_loop(start, done, deep, 0, unroll=4)
    first_half = sublane((depth, rows, width)) < half

    def joined(a, b, place):
        turned_a = pltpu.roll(a, half, 1)
        turned_b = pltpu.roll(b, half, 1)
        low = jnp.where(first_half, a, turned_b).reshape(full, width).astype(BF16)
        high = jnp.where(first_half, turned_a, b).reshape(full, width).astype(BF16)
        out_x[place * full : (place + 1) * full] = jnp.where(odd, high, low)
        out_s[place * full : (place + 1) * full] = jnp.where(odd, low, high)

    joined(now[0, REACH : REACH + depth], now[1, REACH : REACH + depth], 0)
    joined(partial[0], partial[1], 1)
    joined(flat_factor[...], tilt_factor[...], 2)


def inject_kernel(grid_rows, *refs):
    sources, now, (inj, edge_flat, edge_slope), held, (onehot, left, sems) = (
        refs[:4], refs[4], refs[5:8], refs[8:12], refs[12:],
    )
    rc, rt, sc, sw = held
    copies = fetch(sources, held, sems)
    count = rc.shape[1]
    depth, rows, width = edge_flat.shape[1:]
    first_row = lax.axis_index("gy") * rows
    half = rows // 2
    shift = width.bit_length() - 1
    power = 1 << shift == width

    def row_of(cell):
        if power:
            return lax.shift_right_logical(cell, jnp.int32(shift))
        return lax.div(cell, jnp.int32(width))

    own = lax.broadcasted_iota(jnp.int32, (rows, 1), 0)
    own_row = first_row + own
    edge = first_row + jnp.where(own < half, own + rows, own - rows)
    edge_row = jnp.where(
        edge >= grid_rows, edge - grid_rows, jnp.where(edge < 0, edge + grid_rows, edge)
    )

    copies[0].wait()
    copies[1].wait()
    exact = width <= 256
    columns = lax.broadcasted_iota(jnp.int32, (width, LANES), 0)
    if exact:
        columns = columns.astype(F32).astype(BF16)
    one, none = (jnp.ones((), BF16), jnp.zeros((), BF16)) if exact else (1.0, 0.0)
    for start in range(0, count, LANES):
        cells = rc[:, start : start + LANES]
        at_row = row_of(cells)
        at_col = cells - at_row * width
        if exact:
            at_col = at_col.astype(F32).astype(BF16)
        onehot[:, start : start + LANES] = jnp.where(columns == at_col, one, none).astype(BF16)
        parts = []
        for step, wanted in ((0, own_row), (0, edge_row), (1, own_row)):
            amount = rt[step : step + 1, start : start + LANES]
            coarse = amount.astype(BF16).astype(F32)
            fine = amount - coarse
            here = wanted == at_row
            parts.append(jnp.where(here, coarse, 0.0))
            parts.append(jnp.where(here, fine, 0.0))
        left[:, start : start + LANES] = jnp.concatenate(parts, 0).astype(BF16)
    spread = lax.dot_general(
        left[...], onehot[...], (((1,), (1,)), ((), ())), preferred_element_type=F32
    )
    cols = lax.broadcasted_iota(jnp.int32, (rows, width), 1)
    copies[2].wait()
    copies[3].wait()
    for place, (step, wanted) in enumerate(((0, own_row), (0, edge_row), (1, own_row))):
        base = 2 * place * rows
        inj[place, 1] = spread[base : base + rows] + spread[base + rows : base + 2 * rows]
        total = jnp.zeros((rows, width), F32)
        for i in range(sc.shape[0]):
            cell = sc[i]
            at_row = lax.div(cell, jnp.int32(width))
            at_col = cell - at_row * width
            here = jnp.logical_and(wanted == at_row, cols == at_col)
            total = total + jnp.where(here, sw[step, i], 0.0)
        inj[place, 0] = total
    row = sublane((rows, LANES))
    sign = jnp.where(row < half, -1.0, 1.0)
    for m in range(2):
        clear_ends(edge_slope.at[m])

        def edge(z, c, m=m):
            second, first = cross_terms(now[m, z + REACH], row, sign)
            for p in range(width // LANES):
                lanes = slice(p * LANES, (p + 1) * LANES)
                edge_flat[m, z, :, lanes] = second[p]
                edge_slope[m, z + REACH, :, lanes] = first[p]
            return c

        lax.fori_loop(0, depth, edge, 0, unroll=2)


GROUP = 4


def listed(lags, rows, picks):
    count = jnp.int32(0)
    total = lags.shape[0]
    for h in range(total):
        lag = lags[h]
        inside = jnp.logical_and(lag <= rows, lag >= -rows)
        picks[0, count] = lag
        picks[1, count] = h
        count = count + jnp.where(inside, 1, 0)
    for n in range(GROUP):
        picks[0, count + n] = 0
        picks[1, count + n] = total
    return count


def list_rows(counts, picks, entries, shape):
    row = lax.broadcasted_iota(jnp.int32, shape, 0)
    lane = lax.broadcasted_iota(jnp.int32, shape, 1)
    held = jnp.zeros(shape, jnp.int32)
    for n, count in enumerate(counts):
        held = jnp.where(jnp.logical_and(lane == n, row == 2), count, held)
    for n in range(entries):
        value = jnp.where(row == 0, picks[0, n], picks[1, n])
        held = jnp.where(jnp.logical_and(lane == n, row < 2), value, held)
    return held


def listed_far(lags, rows, picks, counts):
    count = jnp.int32(0)
    total = lags.shape[0]
    counts[0] = count
    for size in range(rows + 1, 2 * rows + 1):
        for h in range(total):
            lag = lags[h]
            picks[0, count] = lag
            picks[1, count] = h
            count = count + jnp.where(jnp.logical_or(lag == size, lag == -size), 1, 0)
        counts[size - rows] = count
    for n in range(GROUP):
        picks[0, count + n] = 0
        picks[1, count + n] = total


def read_list(listed_in, picks, entries, counts=0):
    for n in range(counts):
        picks[2, n] = listed_in[2, n]
    for n in range(entries):
        picks[0, n] = listed_in[0, n]
        picks[1, n] = listed_in[1, n]


def table_kernel(
    bins_in, weights_in, lags_in, bins_y, table, near_list, far_list,
    bins, weights, lags, picks, counts, sems,
):
    copies = fetch((bins_in, weights_in, lags_in), (bins, weights, lags), sems)
    rows = bins.shape[1]
    copies[0].wait()
    for y in range(rows):
        bins_y[y] = bins[:, y, :]
    copies[1].wait()
    table_rows, angles, bin_count, lanes = table.shape
    lag_count = table_rows - 1
    table[lag_count] = jnp.zeros((angles, bin_count, lanes), F32)
    values = weights[...].astype(F32)
    for a in range(angles):
        slab = values[:, a, :]
        for h in range(lag_count):
            table[h, a] = jnp.broadcast_to(slab[:, h : h + 1], (bin_count, lanes))
    copies[2].wait()
    count = listed(lags, rows, picks)
    near_list[...] = list_rows((count,), picks, lag_count + GROUP, near_list.shape)
    listed_far(lags, rows, picks, counts)
    far_list[...] = list_rows(
        [counts[n] for n in range(rows + 1)], picks, lag_count + GROUP, far_list.shape
    )


def step_kernel(
    now, sp, partial, flat_factor, tilt_factor, edge_flat, edge_slope, px, ps, inj,
    out, slim, known,
    slope, base, edge_base, edge_tilt, later, later_edge, turned,
):
    depth, rows, width = sp.shape
    half = rows // 2
    full = depth * rows
    odd = is_odd()
    row = sublane((rows, LANES))
    lane = lax.broadcasted_iota(jnp.int32, (rows, LANES), 1)
    sign = jnp.where(row < half, -1.0, 1.0)
    low_half = sublane((rows, width)) < half
    parts = [slice(x, x + LANES) for x in range(0, width, LANES)]
    for m in range(2):
        clear_ends(slope.at[m])
        clear_ends(later.at[m])

    def from_packs(start):
        x = px[pl.ds(start, 2 * rows), :].astype(F32)
        s = ps[pl.ds(start, 2 * rows), :].astype(F32)
        return jnp.where(odd, s, x), jnp.where(odd, x, s)

    def edge_pair(low, high):
        first = jnp.where(low_half, high, row_roll(low, half))
        second = jnp.where(low_half, row_roll(high, half), low)
        return first, second

    def flat(pair, c):
        got = [
            from_packs(pl.multiple_of(n * full + pair * 2 * rows, 2 * rows)) for n in range(3)
        ]
        for j in range(2):
            part = slice(j * rows, (j + 1) * rows)
            z = 2 * pair + j
            edges, partials, factors = [edge_pair(low[part], high[part]) for low, high in got]
            edge_tilt[z] = factors[1]
            for m in range(2):
                edge_base[m, z] = partials[m] + factors[0] * edge_flat[m, z]
                second, first = cross_terms(edges[m], row, sign)
                for p, lanes in enumerate(parts):
                    slope[m, z + REACH, :, lanes] = first[p]
                    base[m, z, :, lanes] = (
                        partial[m, z, :, lanes] + flat_factor[z, :, lanes] * second[p]
                    )
        return c

    lax.fori_loop(0, depth // 2, flat, 0, unroll=2)

    def deep(z, c):
        for m in range(2):
            later[m, z + REACH] = base[m, z] + tilt_factor[z] * depth_first(slope.at[m], z)
            later_edge[m, z] = edge_base[m, z] + edge_tilt[z] * depth_first(edge_slope.at[m], z)
        return c

    lax.fori_loop(0, depth, deep, 0, unroll=4)
    for m in range(2):
        later[m, REACH] = later[m, REACH] + inj[0, m]
        later_edge[m, 0] = later_edge[m, 0] + inj[1, m]

    def flat_later(z, c):
        for m in range(2):
            mid = later[m, z + REACH]
            second, first = flat_terms(mid, later_edge[m, z], row, lane)
            for p, lanes in enumerate(parts):
                slope[m, z + REACH, :, lanes] = first[p]
                base[m, z, :, lanes] = (
                    2.0 * mid[:, lanes]
                    - now[m, z + REACH, :, lanes]
                    + flat_factor[z, :, lanes] * second[p]
                )
                turned[0, m, p, pl.ds(z, rows, stride=depth), :] = mid[:, lanes]
                turned[2, m, p, pl.ds(z, rows, stride=depth), :] = later_edge[m, z, :, lanes]
        return c

    lax.fori_loop(0, depth, flat_later, 0, unroll=4)

    def deep_later(z, c):
        surface = jnp.where(z == 0, 1.0, 0.0)
        for m in range(2):
            value = (
                base[m, z]
                + sp[z] * depth_second(later.at[m], z)
                + tilt_factor[z] * depth_first(slope.at[m], z)
                + surface * inj[2, m]
            )
            for p, lanes in enumerate(parts):
                turned[1, m, p, pl.ds(z, rows, stride=depth), :] = value[:, lanes]
        return c

    lax.fori_loop(0, depth, deep_later, 0, unroll=4)
    kept = jnp.where(odd, 0, half)
    for m in range(2):
        for p, lanes in enumerate(parts):
            for y in range(rows):
                plane = slice(y * depth, (y + 1) * depth)
                out[0, m, y, :, lanes] = turned[0, m, p, plane, :].astype(BF16)
                last = turned[1, m, p, plane, :].astype(BF16)
                out[1, m, y, :, lanes] = last
                slim[(m + 1) * rows + y, :, lanes] = last
            for y in range(half):
                plane = pl.ds(pl.multiple_of((kept + y) * depth, depth), depth)
                slim[m * half + y, :, lanes] = turned[0, m, p, plane, :].astype(BF16)
                known[m, y, :, lanes] = turned[2, m, p, plane, :].astype(BF16)


PAIR = 2


def add_lags(window, table, ids, picks, groups, rows, spots, sums):
    first, end = groups
    steps = window.shape[0]
    angles = table.shape[1]

    def one_group(group, sums):
        sums = [list(a) for a in sums]
        for member in range(GROUP):
            lag = picks[0, group * GROUP + member]
            h = picks[1, group * GROUP + member]
            for n, (y, z, x) in enumerate(spots):
                at = y + 2 * rows
                zs, xs = slice(z, z + 8), slice(x, x + LANES)
                product = None
                for s in range(steps):
                    term = window[s, 0, at - lag, zs, xs] * window[s, 1, at + lag, zs, xs]
                    product = term if product is None else product + term
                for a in range(angles):
                    weight = jnp.take_along_axis(
                        table[h, a], ids[n], axis=0, mode="promise_in_bounds"
                    )
                    sums[a][n] = sums[a][n] + weight * product
        return tuple(tuple(a) for a in sums)

    return lax.fori_loop(first, end, one_group, sums)


def block_of(place):
    return place + jnp.where(is_odd(), 4 - 2 * place, 0)


def place_whole(window, piece, place, rows):
    for s in range(STEPS):
        for m in range(2):
            window[s, m, pl.ds(block_of(place) * rows, rows)] = piece[s, m].astype(F32)


def place_slim(window, slim, known, place, kept, rows):
    half = rows // 2
    start = block_of(place) * rows
    for m in range(2):
        window[0, m, pl.ds(start + kept, half)] = known[m].astype(F32)
        window[0, m, pl.ds(start + half - kept, half)] = slim[
            m * half : (m + 1) * half
        ].astype(F32)
        window[1, m, pl.ds(start, rows)] = slim[(m + 1) * rows : (m + 2) * rows].astype(F32)


def near_image_kernel(near_list, near, known, own, chip, bins, table, out, window, picks):
    rows, depth, width = bins.shape
    angles = table.shape[1]
    read_list(near_list, picks, table.shape[0] - 1 + GROUP)
    groups = (0, lax.div(near_list[2, 0] + (GROUP - 1), GROUP))
    kept = jnp.where(is_odd(), 0, rows // 2)
    place_whole(window, own, 2, rows)
    place_whole(window, chip, 3, rows)
    place_slim(window, near, known, 1, kept, rows)
    tiles = [(z, x) for z in range(0, depth, 8) for x in range(0, width, LANES)]
    zero = jnp.zeros((8, LANES), F32)

    def one_row(y, c):
        ids = [bins[y, z : z + 8, x : x + LANES] for z, x in tiles]
        spots = [(y, z, x) for z, x in tiles]
        sums = tuple((zero,) * len(tiles) for _ in range(angles))
        sums = add_lags(window, table, ids, picks, groups, rows, spots, sums)
        for a in range(angles):
            for n, (z, x) in enumerate(tiles):
                out[a, y, z : z + 8, x : x + LANES] = sums[a][n]
        return c

    lax.fori_loop(0, rows, one_row, 0)


def early_groups(picks, pair, rows):
    inside = jnp.where(is_odd(), rows - PAIR - PAIR * pair, PAIR * pair)
    return lax.div(picks[2, inside], GROUP)


def add_pairs(before, window, table, bins, picks, piece, bounds, store):
    rows, _, width = bins.shape
    angles = table.shape[1]
    tiles = [(piece * 8, x) for x in range(0, width, LANES)]

    def some_rows(pair, c):
        spots = [(PAIR * pair + r, z, x) for r in range(PAIR) for z, x in tiles]
        ids = [bins[y, z : z + 8, x : x + LANES] for y, z, x in spots]
        sums = tuple(
            tuple(before[a, y, z : z + 8, x : x + LANES] for y, z, x in spots)
            for a in range(angles)
        )
        sums = add_lags(window, table, ids, picks, bounds(pair), rows, spots, sums)
        for a in range(angles):
            for n, (y, z, x) in enumerate(spots):
                store(a, y, z, x, sums[a][n])
        return c

    lax.fori_loop(0, rows // PAIR, some_rows, 0)


def mid_image_kernel(
    before_in, far_list, window_in, relay, hint, bins, table, before, window, picks
):
    del before_in, window_in
    rows, depth, _ = bins.shape
    read_list(far_list, picks, table.shape[0] - 1 + GROUP, rows + 1)
    place_slim(window, relay, hint, 4, jnp.where(is_odd(), rows // 2, 0), rows)

    def bounds(pair):
        return 0, early_groups(picks, pair, rows)

    def store(a, y, z, x, value):
        before[a, y, z : z + 8, x : x + LANES] = value

    for piece in range(depth // 8):
        add_pairs(before, window, table, bins, picks, piece, bounds, store)


def far_image_kernel(
    before, far_list, window_in, far, bins, table, out, window, turned, staged, picks, sems
):
    del window_in
    rows, depth, width = bins.shape
    angles = table.shape[1]
    read_list(far_list, picks, table.shape[0] - 1 + GROUP, rows + 1)
    place_whole(window, far, 0, rows)
    last = lax.div(picks[2, rows] + (GROUP - 1), GROUP)

    def bounds(pair):
        return early_groups(picks, pair, rows), last

    def store(a, y, z, x, value):
        turned[a, x // LANES, pl.ds(y, 8, stride=rows), :] = value

    sends = []
    for piece in range(depth // 8):
        add_pairs(before, window, table, bins, picks, piece, bounds, store)
        for a in range(angles):
            for x in range(0, width, LANES):
                staged[piece, a, :, :, x : x + LANES] = (
                    turned[a, x // LANES].astype(BF16).reshape(8, rows, LANES)
                )
        send = pltpu.make_async_copy(
            staged.at[piece], out.at[:, piece * 8 : (piece + 1) * 8], sems.at[piece]
        )
        send.start()
        sends.append(send)
    for send in sends:
        send.wait()


def per_device(
    source_now, source_before, receiver_now, receiver_before, speed_term, aniso_field,
    tilt_field, angle_bins, weight_table, offset_lags, source_cells, source_wavelet,
    receiver_cells, receiver_traces,
):
    depth, rows, width = source_now.shape
    size = lax.axis_size("gy")
    full = depth * rows
    lag_count, bin_count, angles = weight_table.shape
    count = receiver_cells.shape[0]
    parts = width // LANES

    chip_route = [(i, i ^ 1) for i in range(size)]
    near_route = [(i, (i + 1 if i % 2 else i - 1) % size) for i in range(size)]

    def moved(block, route):
        return lax.ppermute(block, "gy", route)

    fields = (
        source_now, source_before, receiver_now, receiver_before, speed_term, aniso_field,
        tilt_field,
    )
    tall = depth + 2 * REACH
    grid = (depth, rows, width)
    pack_shape = jax.ShapeDtypeStruct((3 * full, width), BF16)
    pack_x, pack_s, now, speed, partial, flat_factor, tilt_factor = call(
        pack_kernel,
        [
            pack_shape,
            pack_shape,
            jax.ShapeDtypeStruct((2, tall, rows, width), F32),
            jax.ShapeDtypeStruct(grid, F32),
            jax.ShapeDtypeStruct((2,) + grid, F32),
            jax.ShapeDtypeStruct(grid, F32),
            jax.ShapeDtypeStruct(grid, F32),
        ],
        [HBM] * 7,
        [pltpu.VMEM(grid, F32)] * 4
        + [
            pltpu.VMEM((2, tall, rows, width), F32),
            pltpu.VMEM((2,) + grid, F32),
            pltpu.SemaphoreType.DMA((4, 7)),
        ],
        8,
        full * width * 200,
        full * width * 40,
    )(*in_hbm(fields))
    got_s = moved(pack_s, chip_route)
    got_x = moved(pack_x, near_route)

    inj, edge_flat, edge_slope = call(
        functools.partial(inject_kernel, size * rows),
        [
            jax.ShapeDtypeStruct((3, 2, rows, width), F32),
            jax.ShapeDtypeStruct((2,) + grid, F32),
            jax.ShapeDtypeStruct((2, tall, rows, width), F32),
        ],
        [HBM] * 4 + [VMEM],
        [
            pltpu.VMEM((1, count), jnp.int32),
            pltpu.VMEM((STEPS, count), F32),
            pltpu.SMEM(source_cells.shape, jnp.int32),
            pltpu.SMEM(source_wavelet.shape, F32),
            pltpu.VMEM((width, count), BF16),
            pltpu.VMEM((6 * rows, count), BF16),
            pltpu.SemaphoreType.DMA((4,)),
        ],
        8,
        12 * rows * count * width,
        full * width * 8,
    )(
        *in_hbm((receiver_cells[None], receiver_traces, source_cells, source_wavelet)),
        now,
    )
    pick_space = pltpu.SMEM((8, LANES), jnp.int32)
    bins_y, table, near_list, far_list = call(
        table_kernel,
        [
            jax.ShapeDtypeStruct((rows, depth, width), jnp.int32),
            jax.ShapeDtypeStruct((lag_count + 1, angles, bin_count, LANES), F32),
            jax.ShapeDtypeStruct((8, LANES), jnp.int32),
            jax.ShapeDtypeStruct((8, LANES), jnp.int32),
        ],
        [HBM] * 3,
        [
            pltpu.VMEM(grid, jnp.int32),
            pltpu.VMEM((bin_count, angles, lag_count), BF16),
            pltpu.SMEM(offset_lags.shape, jnp.int32),
            pick_space,
            pltpu.SMEM((rows + 1,), jnp.int32),
            pltpu.SemaphoreType.DMA((3,)),
        ],
        8,
        full * width,
        full * width * 8,
    )(*in_hbm((angle_bins, jnp.transpose(weight_table, (1, 2, 0)), offset_lags)))

    half = rows // 2
    own, slim, known = call(
        step_kernel,
        [
            jax.ShapeDtypeStruct((STEPS, 2, rows, depth, width), BF16),
            jax.ShapeDtypeStruct((2 * (half + rows), depth, width), BF16),
            jax.ShapeDtypeStruct((2, half, depth, width), BF16),
        ],
        [VMEM] * 10,
        [
            pltpu.VMEM((2, tall, rows, width), F32),
            pltpu.VMEM((2,) + grid, F32),
            pltpu.VMEM((2,) + grid, F32),
            pltpu.VMEM(grid, F32),
            pltpu.VMEM((2, tall, rows, width), F32),
            pltpu.VMEM((2,) + grid, F32),
            pltpu.VMEM((STEPS + 1, 2, parts, full, LANES), F32),
        ],
        16,
        full * width * 300,
        full * width * 50,
    )(
        now, speed, partial, flat_factor, tilt_factor, edge_flat, edge_slope, got_x, got_s, inj,
    )

    chip = moved(own, chip_route)
    near = moved(slim, near_route)
    far = moved(chip, near_route)
    hint = moved(known, chip_route)
    relay = moved(near, chip_route)
    window_shape = jax.ShapeDtypeStruct((STEPS, 2, 5 * rows, depth, width), F32)
    half_image, window = call(
        near_image_kernel,
        [jax.ShapeDtypeStruct((angles, rows, depth, width), F32), window_shape],
        [VMEM] * 7,
        [pick_space],
        16,
        full * width * lag_count * 6,
        full * width * 20,
    )(near_list, near, known, own, chip, bins_y, table)
    half_image, window = call(
        mid_image_kernel,
        [jax.ShapeDtypeStruct((angles, rows, depth, width), F32), window_shape],
        [VMEM] * 7,
        [pick_space],
        16,
        full * width * lag_count * 3,
        full * width * 20,
        None,
        {0: 0, 2: 1},
    )(half_image, far_list, window, relay, hint, bins_y, table)
    pieces = depth // 8
    return call(
        far_image_kernel,
        [jax.ShapeDtypeStruct((angles, depth, rows, width), BF16), window_shape],
        [VMEM] * 6,
        [
            pltpu.VMEM((angles, parts, 8 * rows, LANES), F32),
            pltpu.VMEM((pieces, angles, 8, rows, width), BF16),
            pick_space,
            pltpu.SemaphoreType.DMA((pieces,)),
        ],
        16,
        full * width * lag_count * 3,
        full * width * 20,
        [HBM, VMEM],
        {2: 1},
    )(half_image, far_list, window, far, bins_y, table)[0]


def solution(mesh):
    grid = P("shot", "gy", None)
    media = P(None, "gy", None)
    return jax.shard_map(
        per_device,
        mesh=mesh,
        in_specs=(grid,) * 4
        + (media,) * 4
        + (P(), P(), P("shot"), P("shot", None), P("shot"), P("shot", None)),
        out_specs=P("shot", None, "gy", None),
        check_vma=False,
    )
```

```python
import functools

import jax
import jax.numpy as jnp
from jax import lax
from jax.experimental import pallas as pl
from jax.experimental.pallas import tpu as pltpu
from jax.sharding import PartitionSpec as P


STEPS = 2
SECOND = (-205.0 / 72.0, 8.0 / 5.0, -1.0 / 5.0, 8.0 / 315.0, -1.0 / 560.0)
FIRST = (4.0 / 5.0, -1.0 / 5.0, 4.0 / 105.0, -1.0 / 280.0)
REACH = 4
LANES = 128
F32 = jnp.float32
BF16 = jnp.bfloat16

VMEM = pl.BlockSpec(memory_space=pltpu.VMEM)
HBM = pl.BlockSpec(memory_space=pltpu.HBM)


def in_hbm(arrays):
    return [pltpu.with_memory_space_constraint(array, pltpu.HBM) for array in arrays]


def fetch(sources, targets, sems):
    copies = [
        pltpu.make_async_copy(source, target, sems.at[n])
        for n, (source, target) in enumerate(zip(sources, targets))
    ]
    for copy in copies:
        copy.start()
    return copies


def call(kernel, outs, in_specs, scratch, mib, flops, bytes_moved, places=None, aliases=None):
    return pl.pallas_call(
        kernel,
        out_shape=outs,
        in_specs=in_specs,
        out_specs=places or [VMEM] * len(outs),
        input_output_aliases=aliases or {},
        scratch_shapes=scratch,
        compiler_params=pltpu.CompilerParams(vmem_limit_bytes=mib << 20),
        cost_estimate=pl.CostEstimate(
            flops=flops, bytes_accessed=bytes_moved, transcendentals=0
        ),
    )


def is_odd():
    return lax.axis_index("gy") % 2 == 1


def sublane(shape):
    return lax.broadcasted_iota(jnp.int32, shape, len(shape) - 2)


def lane_parts(value):
    return [value[:, x : x + LANES] for x in range(0, value.shape[1], LANES)]


def row_roll(value, k):
    return pltpu.roll(value, k % value.shape[0], 0)


def flat_terms(value, edge, row, lane):
    parts = lane_parts(value)
    edges = None if edge is None else lane_parts(edge)
    rows = value.shape[0]
    second = [(2.0 * SECOND[0]) * part for part in parts]
    first = [None] * len(parts)
    for k in range(1, REACH + 1):
        right = [pltpu.roll(part, k, 1) for part in parts]
        left = [pltpu.roll(part, LANES - k, 1) for part in parts]
        for p, part in enumerate(parts):
            below = jnp.where(lane >= k, right[p], right[p - 1] if p else 0.0)
            above = jnp.where(lane < LANES - k, left[p], left[p + 1] if p + 1 < len(parts) else 0.0)
            outer_up = 0.0 if edges is None else row_roll(edges[p], -k)
            outer_down = 0.0 if edges is None else row_roll(edges[p], k)
            up = jnp.where(row < rows - k, row_roll(part, -k), outer_up)
            down = jnp.where(row >= k, row_roll(part, k), outer_down)
            ahead, behind = above + up, below + down
            second[p] = second[p] + SECOND[k] * (ahead + behind)
            term = FIRST[k - 1] * (ahead - behind)
            first[p] = term if first[p] is None else first[p] + term
    return second, first


def cross_terms(edge, row, sign):
    rows = edge.shape[0]
    second, first = [], []
    for part in lane_parts(edge):
        a = b = None
        for k in range(1, REACH + 1):
            value = jnp.where(
                row < k, row_roll(part, k), jnp.where(row >= rows - k, row_roll(part, -k), 0.0)
            )
            a = SECOND[k] * value if a is None else a + SECOND[k] * value
            b = FIRST[k - 1] * value if b is None else b + FIRST[k - 1] * value
        second.append(a)
        first.append(sign * b)
    return second, first


def depth_second(field, at):
    second = SECOND[0] * field[at + REACH]
    for k in range(1, REACH + 1):
        second = second + SECOND[k] * (field[at + REACH + k] + field[at + REACH - k])
    return second


def depth_first(slope, at):
    first = None
    for k in range(1, REACH + 1):
        term = FIRST[k - 1] * (slope[at + REACH + k] - slope[at + REACH - k])
        first = term if first is None else first + term
    return first


def clear_ends(ref):
    depth = ref.shape[0] - 2 * REACH
    zeros = jnp.zeros((REACH,) + ref.shape[1:], F32)
    ref[:REACH] = zeros
    ref[REACH + depth :] = zeros


def pack_kernel(*refs):
    sources, (out_x, out_s, now, sp, partial, flat_factor, tilt_factor), rest = (
        refs[:7], refs[7:14], refs[14:],
    )
    (sb, rb, an, ti, slope, base), sems = rest[:6], rest[6]
    sn, rn = now.at[0], now.at[1]
    depth, rows, width = sp.shape
    half = rows // 2
    full = depth * rows
    odd = is_odd()
    row = sublane((rows, LANES))
    lane = lax.broadcasted_iota(jnp.int32, (rows, LANES), 1)
    order = (0, 2, 1, 3, 4, 5, 6)
    chunks = 4
    chunk = depth // chunks
    inner = pl.ds(REACH, depth)
    targets = (sn.at[inner], rn.at[inner], sb, rb, sp, an, ti)
    copies = []
    for c in range(chunks):
        span = pl.ds(c * chunk, chunk)
        copies.append(
            fetch(
                [sources[n].at[span] for n in order],
                [target.at[span] for target in targets],
                sems.at[c],
            )
        )
    for ref in (sn, rn):
        clear_ends(ref)
    for m in range(2):
        clear_ends(slope.at[m])

    def flat(z, c):
        factor = sp[z] * (1.0 + 2.0 * an[z])
        flat_factor[z] = factor
        tilt_factor[z] = sp[z] * ti[z]
        for m, before in enumerate((sb, rb)):
            value = now[m, z + REACH]
            second, first = flat_terms(value, None, row, lane)
            for p in range(width // LANES):
                lanes = slice(p * LANES, (p + 1) * LANES)
                slope[m, z + REACH, :, lanes] = first[p]
                base[m, z, :, lanes] = (
                    2.0 * value[:, lanes] - before[z, :, lanes] + factor[:, lanes] * second[p]
                )
        return c

    def deep(z, c):
        for m in range(2):
            partial[m, z] = (
                base[m, z]
                + sp[z] * depth_second(now.at[m], z)
                + tilt_factor[z] * depth_first(slope.at[m], z)
            )
        return c

    for c in range(chunks):
        for copy in copies[c]:
            copy.wait()
        lax.fori_loop(c * chunk, (c + 1) * chunk, flat, 0, unroll=4)
        done = (c + 1) * chunk if c == chunks - 1 else max((c + 1) * chunk - REACH, 0)
        start = max(c * chunk - REACH, 0)
        if done > start:
            lax.fori_loop(start, done, deep, 0, unroll=4)
    first_half = sublane((depth, rows, width)) < half

    def joined(a, b, place):
        turned_a = pltpu.roll(a, half, 1)
        turned_b = pltpu.roll(b, half, 1)
        low = jnp.where(first_half, a, turned_b).reshape(full, width).astype(BF16)
        high = jnp.where(first_half, turned_a, b).reshape(full, width).astype(BF16)
        out_x[place * full : (place + 1) * full] = jnp.where(odd, high, low)
        out_s[place * full : (place + 1) * full] = jnp.where(odd, low, high)

    joined(now[0, REACH : REACH + depth], now[1, REACH : REACH + depth], 0)
    joined(partial[0], partial[1], 1)
    joined(flat_factor[...], tilt_factor[...], 2)


def inject_kernel(grid_rows, *refs):
    sources, now, (inj, edge_flat, edge_slope), held, (onehot, left, sems) = (
        refs[:4], refs[4], refs[5:8], refs[8:12], refs[12:],
    )
    rc, rt, sc, sw = held
    copies = fetch(sources, held, sems)
    count = rc.shape[1]
    depth, rows, width = edge_flat.shape[1:]
    first_row = lax.axis_index("gy") * rows
    half = rows // 2
    shift = width.bit_length() - 1
    power = 1 << shift == width

    def row_of(cell):
        if power:
            return lax.shift_right_logical(cell, jnp.int32(shift))
        return lax.div(cell, jnp.int32(width))

    own = lax.broadcasted_iota(jnp.int32, (rows, 1), 0)
    own_row = first_row + own
    edge = first_row + jnp.where(own < half, own + rows, own - rows)
    edge_row = jnp.where(
        edge >= grid_rows, edge - grid_rows, jnp.where(edge < 0, edge + grid_rows, edge)
    )

    copies[0].wait()
    copies[1].wait()
    exact = width <= 256
    columns = lax.broadcasted_iota(jnp.int32, (width, LANES), 0)
    if exact:
        columns = columns.astype(F32).astype(BF16)
    one, none = (jnp.ones((), BF16), jnp.zeros((), BF16)) if exact else (1.0, 0.0)
    for start in range(0, count, LANES):
        cells = rc[:, start : start + LANES]
        at_row = row_of(cells)
        at_col = cells - at_row * width
        if exact:
            at_col = at_col.astype(F32).astype(BF16)
        onehot[:, start : start + LANES] = jnp.where(columns == at_col, one, none).astype(BF16)
        parts = []
        for step, wanted in ((0, own_row), (0, edge_row), (1, own_row)):
            amount = rt[step : step + 1, start : start + LANES]
            coarse = amount.astype(BF16).astype(F32)
            fine = amount - coarse
            here = wanted == at_row
            parts.append(jnp.where(here, coarse, 0.0))
            parts.append(jnp.where(here, fine, 0.0))
        left[:, start : start + LANES] = jnp.concatenate(parts, 0).astype(BF16)
    spread = lax.dot_general(
        left[...], onehot[...], (((1,), (1,)), ((), ())), preferred_element_type=F32
    )
    cols = lax.broadcasted_iota(jnp.int32, (rows, width), 1)
    copies[2].wait()
    copies[3].wait()
    for place, (step, wanted) in enumerate(((0, own_row), (0, edge_row), (1, own_row))):
        base = 2 * place * rows
        inj[place, 1] = spread[base : base + rows] + spread[base + rows : base + 2 * rows]
        total = jnp.zeros((rows, width), F32)
        for i in range(sc.shape[0]):
            cell = sc[i]
            at_row = lax.div(cell, jnp.int32(width))
            at_col = cell - at_row * width
            here = jnp.logical_and(wanted == at_row, cols == at_col)
            total = total + jnp.where(here, sw[step, i], 0.0)
        inj[place, 0] = total
    row = sublane((rows, LANES))
    sign = jnp.where(row < half, -1.0, 1.0)
    for m in range(2):
        clear_ends(edge_slope.at[m])

        def edge(z, c, m=m):
            second, first = cross_terms(now[m, z + REACH], row, sign)
            for p in range(width // LANES):
                lanes = slice(p * LANES, (p + 1) * LANES)
                edge_flat[m, z, :, lanes] = second[p]
                edge_slope[m, z + REACH, :, lanes] = first[p]
            return c

        lax.fori_loop(0, depth, edge, 0, unroll=2)


GROUP = 4


def listed(lags, rows, picks):
    count = jnp.int32(0)
    total = lags.shape[0]
    for h in range(total):
        lag = lags[h]
        inside = jnp.logical_and(lag <= rows, lag >= -rows)
        picks[0, count] = lag
        picks[1, count] = h
        count = count + jnp.where(inside, 1, 0)
    for n in range(GROUP):
        picks[0, count + n] = 0
        picks[1, count + n] = total
    return count


def list_rows(counts, picks, entries, shape):
    row = lax.broadcasted_iota(jnp.int32, shape, 0)
    lane = lax.broadcasted_iota(jnp.int32, shape, 1)
    held = jnp.zeros(shape, jnp.int32)
    for n, count in enumerate(counts):
        held = jnp.where(jnp.logical_and(lane == n, row == 2), count, held)
    for n in range(entries):
        value = jnp.where(row == 0, picks[0, n], picks[1, n])
        held = jnp.where(jnp.logical_and(lane == n, row < 2), value, held)
    return held


def listed_far(lags, rows, picks, counts):
    count = jnp.int32(0)
    total = lags.shape[0]
    counts[0] = count
    for size in range(rows + 1, 2 * rows + 1):
        for h in range(total):
            lag = lags[h]
            picks[0, count] = lag
            picks[1, count] = h
            count = count + jnp.where(jnp.logical_or(lag == size, lag == -size), 1, 0)
        counts[size - rows] = count
    for n in range(GROUP):
        picks[0, count + n] = 0
        picks[1, count + n] = total


def read_list(listed_in, picks, entries, counts=0):
    for n in range(counts):
        picks[2, n] = listed_in[2, n]
    for n in range(entries):
        picks[0, n] = listed_in[0, n]
        picks[1, n] = listed_in[1, n]


def table_kernel(
    bins_in, weights_in, lags_in, bins_y, table, near_list, far_list,
    bins, weights, lags, picks, counts, sems,
):
    copies = fetch((bins_in, weights_in, lags_in), (bins, weights, lags), sems)
    rows = bins.shape[1]
    copies[0].wait()
    for y in range(rows):
        bins_y[y] = bins[:, y, :]
    copies[1].wait()
    table_rows, angles, bin_count, lanes = table.shape
    lag_count = table_rows - 1
    table[lag_count] = jnp.zeros((angles, bin_count, lanes), F32)
    values = weights[...].astype(F32)
    for a in range(angles):
        slab = values[:, a, :]
        for h in range(lag_count):
            table[h, a] = jnp.broadcast_to(slab[:, h : h + 1], (bin_count, lanes))
    copies[2].wait()
    count = listed(lags, rows, picks)
    near_list[...] = list_rows((count,), picks, lag_count + GROUP, near_list.shape)
    listed_far(lags, rows, picks, counts)
    far_list[...] = list_rows(
        [counts[n] for n in range(rows + 1)], picks, lag_count + GROUP, far_list.shape
    )


def step_kernel(
    now, sp, partial, flat_factor, tilt_factor, edge_flat, edge_slope, px, ps, inj,
    out, slim, known,
    slope, base, edge_base, edge_tilt, later, later_edge, turned,
):
    depth, rows, width = sp.shape
    half = rows // 2
    full = depth * rows
    odd = is_odd()
    row = sublane((rows, LANES))
    lane = lax.broadcasted_iota(jnp.int32, (rows, LANES), 1)
    sign = jnp.where(row < half, -1.0, 1.0)
    low_half = sublane((rows, width)) < half
    parts = [slice(x, x + LANES) for x in range(0, width, LANES)]
    for m in range(2):
        clear_ends(slope.at[m])
        clear_ends(later.at[m])

    def from_packs(start):
        x = px[pl.ds(start, 2 * rows), :].astype(F32)
        s = ps[pl.ds(start, 2 * rows), :].astype(F32)
        return jnp.where(odd, s, x), jnp.where(odd, x, s)

    def edge_pair(low, high):
        first = jnp.where(low_half, high, row_roll(low, half))
        second = jnp.where(low_half, row_roll(high, half), low)
        return first, second

    def flat(pair, c):
        got = [
            from_packs(pl.multiple_of(n * full + pair * 2 * rows, 2 * rows)) for n in range(3)
        ]
        for j in range(2):
            part = slice(j * rows, (j + 1) * rows)
            z = 2 * pair + j
            edges, partials, factors = [edge_pair(low[part], high[part]) for low, high in got]
            edge_tilt[z] = factors[1]
            for m in range(2):
                edge_base[m, z] = partials[m] + factors[0] * edge_flat[m, z]
                second, first = cross_terms(edges[m], row, sign)
                for p, lanes in enumerate(parts):
                    slope[m, z + REACH, :, lanes] = first[p]
                    base[m, z, :, lanes] = (
                        partial[m, z, :, lanes] + flat_factor[z, :, lanes] * second[p]
                    )
        return c

    lax.fori_loop(0, depth // 2, flat, 0, unroll=4)

    def deep(z, c):
        for m in range(2):
            later[m, z + REACH] = base[m, z] + tilt_factor[z] * depth_first(slope.at[m], z)
            later_edge[m, z] = edge_base[m, z] + edge_tilt[z] * depth_first(edge_slope.at[m], z)
        return c

    lax.fori_loop(0, depth, deep, 0, unroll=8)
    for m in range(2):
        later[m, REACH] = later[m, REACH] + inj[0, m]
        later_edge[m, 0] = later_edge[m, 0] + inj[1, m]

    def flat_later(z, c):
        for m in range(2):
            mid = later[m, z + REACH]
            second, first = flat_terms(mid, later_edge[m, z], row, lane)
            for p, lanes in enumerate(parts):
                slope[m, z + REACH, :, lanes] = first[p]
                base[m, z, :, lanes] = (
                    2.0 * mid[:, lanes]
                    - now[m, z + REACH, :, lanes]
                    + flat_factor[z, :, lanes] * second[p]
                )
                turned[0, m, p, pl.ds(z, rows, stride=depth), :] = mid[:, lanes]
                turned[2, m, p, pl.ds(z, rows, stride=depth), :] = later_edge[m, z, :, lanes]
        return c

    lax.fori_loop(0, depth, flat_later, 0, unroll=8)

    def deep_later(z, c):
        surface = jnp.where(z == 0, 1.0, 0.0)
        for m in range(2):
            value = (
                base[m, z]
                + sp[z] * depth_second(later.at[m], z)
                + tilt_factor[z] * depth_first(slope.at[m], z)
                + surface * inj[2, m]
            )
            for p, lanes in enumerate(parts):
                turned[1, m, p, pl.ds(z, rows, stride=depth), :] = value[:, lanes]
        return c

    lax.fori_loop(0, depth, deep_later, 0, unroll=8)
    kept = jnp.where(odd, 0, half)
    for m in range(2):
        for p, lanes in enumerate(parts):
            for y in range(rows):
                plane = slice(y * depth, (y + 1) * depth)
                out[0, m, y, :, lanes] = turned[0, m, p, plane, :].astype(BF16)
                last = turned[1, m, p, plane, :].astype(BF16)
                out[1, m, y, :, lanes] = last
                slim[(m + 1) * rows + y, :, lanes] = last
            for y in range(half):
                plane = pl.ds(pl.multiple_of((kept + y) * depth, depth), depth)
                slim[m * half + y, :, lanes] = turned[0, m, p, plane, :].astype(BF16)
                known[m, y, :, lanes] = turned[2, m, p, plane, :].astype(BF16)


PAIR = 4


def add_lags(window, table, ids, picks, groups, rows, spots, sums):
    first, end = groups
    steps = window.shape[0]
    angles = table.shape[1]

    def one_group(group, sums):
        sums = [list(a) for a in sums]
        for member in range(GROUP):
            lag = picks[0, group * GROUP + member]
            h = picks[1, group * GROUP + member]
            for n, (y, z, x) in enumerate(spots):
                at = y + 2 * rows
                zs, xs = slice(z, z + 8), slice(x, x + LANES)
                product = None
                for s in range(steps):
                    term = window[s, 0, at - lag, zs, xs] * window[s, 1, at + lag, zs, xs]
                    product = term if product is None else product + term
                for a in range(angles):
                    weight = jnp.take_along_axis(
                        table[h, a], ids[n], axis=0, mode="promise_in_bounds"
                    )
                    sums[a][n] = sums[a][n] + weight * product
        return tuple(tuple(a) for a in sums)

    return lax.fori_loop(first, end, one_group, sums)


def block_of(place):
    return place + jnp.where(is_odd(), 4 - 2 * place, 0)


def place_whole(window, piece, place, rows):
    for s in range(STEPS):
        for m in range(2):
            window[s, m, pl.ds(block_of(place) * rows, rows)] = piece[s, m].astype(F32)


def place_slim(window, slim, known, place, kept, rows):
    half = rows // 2
    start = block_of(place) * rows
    for m in range(2):
        window[0, m, pl.ds(start + kept, half)] = known[m].astype(F32)
        window[0, m, pl.ds(start + half - kept, half)] = slim[
            m * half : (m + 1) * half
        ].astype(F32)
        window[1, m, pl.ds(start, rows)] = slim[(m + 1) * rows : (m + 2) * rows].astype(F32)


def near_image_kernel(near_list, near, known, own, chip, bins, table, out, window, picks):
    rows, depth, width = bins.shape
    angles = table.shape[1]
    read_list(near_list, picks, table.shape[0] - 1 + GROUP)
    groups = (0, lax.div(near_list[2, 0] + (GROUP - 1), GROUP))
    kept = jnp.where(is_odd(), 0, rows // 2)
    place_whole(window, own, 2, rows)
    place_whole(window, chip, 3, rows)
    place_slim(window, near, known, 1, kept, rows)
    tiles = [(z, x) for z in range(0, depth, 8) for x in range(0, width, LANES)]
    zero = jnp.zeros((8, LANES), F32)

    def one_row(y, c):
        ids = [bins[y, z : z + 8, x : x + LANES] for z, x in tiles]
        spots = [(y, z, x) for z, x in tiles]
        sums = tuple((zero,) * len(tiles) for _ in range(angles))
        sums = add_lags(window, table, ids, picks, groups, rows, spots, sums)
        for a in range(angles):
            for n, (z, x) in enumerate(tiles):
                out[a, y, z : z + 8, x : x + LANES] = sums[a][n]
        return c

    lax.fori_loop(0, rows, one_row, 0)


def early_groups(picks, pair, rows):
    inside = jnp.where(is_odd(), rows - PAIR - PAIR * pair, PAIR * pair)
    return lax.div(picks[2, inside], GROUP)


def add_pairs(before, window, table, bins, picks, piece, bounds, store):
    rows, _, width = bins.shape
    angles = table.shape[1]
    tiles = [(piece * 8, x) for x in range(0, width, LANES)]

    def some_rows(pair, c):
        spots = [(PAIR * pair + r, z, x) for r in range(PAIR) for z, x in tiles]
        ids = [bins[y, z : z + 8, x : x + LANES] for y, z, x in spots]
        sums = tuple(
            tuple(before[a, y, z : z + 8, x : x + LANES] for y, z, x in spots)
            for a in range(angles)
        )
        sums = add_lags(window, table, ids, picks, bounds(pair), rows, spots, sums)
        for a in range(angles):
            for n, (y, z, x) in enumerate(spots):
                store(a, y, z, x, sums[a][n])
        return c

    lax.fori_loop(0, rows // PAIR, some_rows, 0)


def mid_image_kernel(
    before_in, far_list, window_in, relay, hint, bins, table, before, window, picks
):
    del before_in, window_in
    rows, depth, _ = bins.shape
    read_list(far_list, picks, table.shape[0] - 1 + GROUP, rows + 1)
    place_slim(window, relay, hint, 4, jnp.where(is_odd(), rows // 2, 0), rows)

    def bounds(pair):
        return 0, early_groups(picks, pair, rows)

    def store(a, y, z, x, value):
        before[a, y, z : z + 8, x : x + LANES] = value

    for piece in range(depth // 8):
        add_pairs(before, window, table, bins, picks, piece, bounds, store)


def far_image_kernel(
    before, far_list, window_in, far, bins, table, out, window, turned, staged, picks, sems
):
    del window_in
    rows, depth, width = bins.shape
    angles = table.shape[1]
    read_list(far_list, picks, table.shape[0] - 1 + GROUP, rows + 1)
    place_whole(window, far, 0, rows)
    last = lax.div(picks[2, rows] + (GROUP - 1), GROUP)

    def bounds(pair):
        return early_groups(picks, pair, rows), last

    def store(a, y, z, x, value):
        turned[a, x // LANES, pl.ds(y, 8, stride=rows), :] = value

    sends = []
    for piece in range(depth // 8):
        add_pairs(before, window, table, bins, picks, piece, bounds, store)
        for a in range(angles):
            for x in range(0, width, LANES):
                staged[piece, a, :, :, x : x + LANES] = (
                    turned[a, x // LANES].astype(BF16).reshape(8, rows, LANES)
                )
        send = pltpu.make_async_copy(
            staged.at[piece], out.at[:, piece * 8 : (piece + 1) * 8], sems.at[piece]
        )
        send.start()
        sends.append(send)
    for send in sends:
        send.wait()


def per_device(
    source_now, source_before, receiver_now, receiver_before, speed_term, aniso_field,
    tilt_field, angle_bins, weight_table, offset_lags, source_cells, source_wavelet,
    receiver_cells, receiver_traces,
):
    depth, rows, width = source_now.shape
    size = lax.axis_size("gy")
    full = depth * rows
    lag_count, bin_count, angles = weight_table.shape
    count = receiver_cells.shape[0]
    parts = width // LANES

    chip_route = [(i, i ^ 1) for i in range(size)]
    near_route = [(i, (i + 1 if i % 2 else i - 1) % size) for i in range(size)]

    def moved(block, route):
        return lax.ppermute(block, "gy", route)

    fields = (
        source_now, source_before, receiver_now, receiver_before, speed_term, aniso_field,
        tilt_field,
    )
    tall = depth + 2 * REACH
    grid = (depth, rows, width)
    pack_shape = jax.ShapeDtypeStruct((3 * full, width), BF16)
    pack_x, pack_s, now, speed, partial, flat_factor, tilt_factor = call(
        pack_kernel,
        [
            pack_shape,
            pack_shape,
            jax.ShapeDtypeStruct((2, tall, rows, width), F32),
            jax.ShapeDtypeStruct(grid, F32),
            jax.ShapeDtypeStruct((2,) + grid, F32),
            jax.ShapeDtypeStruct(grid, F32),
            jax.ShapeDtypeStruct(grid, F32),
        ],
        [HBM] * 7,
        [pltpu.VMEM(grid, F32)] * 4
        + [
            pltpu.VMEM((2, tall, rows, width), F32),
            pltpu.VMEM((2,) + grid, F32),
            pltpu.SemaphoreType.DMA((4, 7)),
        ],
        8,
        full * width * 200,
        full * width * 40,
    )(*in_hbm(fields))
    got_s = moved(pack_s, chip_route)
    got_x = moved(pack_x, near_route)

    inj, edge_flat, edge_slope = call(
        functools.partial(inject_kernel, size * rows),
        [
            jax.ShapeDtypeStruct((3, 2, rows, width), F32),
            jax.ShapeDtypeStruct((2,) + grid, F32),
            jax.ShapeDtypeStruct((2, tall, rows, width), F32),
        ],
        [HBM] * 4 + [VMEM],
        [
            pltpu.VMEM((1, count), jnp.int32),
            pltpu.VMEM((STEPS, count), F32),
            pltpu.SMEM(source_cells.shape, jnp.int32),
            pltpu.SMEM(source_wavelet.shape, F32),
            pltpu.VMEM((width, count), BF16),
            pltpu.VMEM((6 * rows, count), BF16),
            pltpu.SemaphoreType.DMA((4,)),
        ],
        8,
        12 * rows * count * width,
        full * width * 8,
    )(
        *in_hbm((receiver_cells[None], receiver_traces, source_cells, source_wavelet)),
        now,
    )
    pick_space = pltpu.SMEM((8, LANES), jnp.int32)
    bins_y, table, near_list, far_list = call(
        table_kernel,
        [
            jax.ShapeDtypeStruct((rows, depth, width), jnp.int32),
            jax.ShapeDtypeStruct((lag_count + 1, angles, bin_count, LANES), F32),
            jax.ShapeDtypeStruct((8, LANES), jnp.int32),
            jax.ShapeDtypeStruct((8, LANES), jnp.int32),
        ],
        [HBM] * 3,
        [
            pltpu.VMEM(grid, jnp.int32),
            pltpu.VMEM((bin_count, angles, lag_count), BF16),
            pltpu.SMEM(offset_lags.shape, jnp.int32),
            pick_space,
            pltpu.SMEM((rows + 1,), jnp.int32),
            pltpu.SemaphoreType.DMA((3,)),
        ],
        8,
        full * width,
        full * width * 8,
    )(*in_hbm((angle_bins, jnp.transpose(weight_table, (1, 2, 0)), offset_lags)))

    half = rows // 2
    own, slim, known = call(
        step_kernel,
        [
            jax.ShapeDtypeStruct((STEPS, 2, rows, depth, width), BF16),
            jax.ShapeDtypeStruct((2 * (half + rows), depth, width), BF16),
            jax.ShapeDtypeStruct((2, half, depth, width), BF16),
        ],
        [VMEM] * 10,
        [
            pltpu.VMEM((2, tall, rows, width), F32),
            pltpu.VMEM((2,) + grid, F32),
            pltpu.VMEM((2,) + grid, F32),
            pltpu.VMEM(grid, F32),
            pltpu.VMEM((2, tall, rows, width), F32),
            pltpu.VMEM((2,) + grid, F32),
            pltpu.VMEM((STEPS + 1, 2, parts, full, LANES), F32),
        ],
        16,
        full * width * 300,
        full * width * 50,
    )(
        now, speed, partial, flat_factor, tilt_factor, edge_flat, edge_slope, got_x, got_s, inj,
    )

    chip = moved(own, chip_route)
    near = moved(slim, near_route)
    far = moved(chip, near_route)
    hint = moved(known, chip_route)
    relay = moved(near, chip_route)
    window_shape = jax.ShapeDtypeStruct((STEPS, 2, 5 * rows, depth, width), F32)
    half_image, window = call(
        near_image_kernel,
        [jax.ShapeDtypeStruct((angles, rows, depth, width), F32), window_shape],
        [VMEM] * 7,
        [pick_space],
        16,
        full * width * lag_count * 6,
        full * width * 20,
    )(near_list, near, known, own, chip, bins_y, table)
    half_image, window = call(
        mid_image_kernel,
        [jax.ShapeDtypeStruct((angles, rows, depth, width), F32), window_shape],
        [VMEM] * 7,
        [pick_space],
        16,
        full * width * lag_count * 3,
        full * width * 20,
        None,
        {0: 0, 2: 1},
    )(half_image, far_list, window, relay, hint, bins_y, table)
    pieces = depth // 8
    return call(
        far_image_kernel,
        [jax.ShapeDtypeStruct((angles, depth, rows, width), BF16), window_shape],
        [VMEM] * 6,
        [
            pltpu.VMEM((angles, parts, 8 * rows, LANES), F32),
            pltpu.VMEM((pieces, angles, 8, rows, width), BF16),
            pick_space,
            pltpu.SemaphoreType.DMA((pieces,)),
        ],
        16,
        full * width * lag_count * 3,
        full * width * 20,
        [HBM, VMEM],
        {2: 1},
    )(half_image, far_list, window, far, bins_y, table)[0]


def solution(mesh):
    grid = P("shot", "gy", None)
    media = P(None, "gy", None)
    return jax.shard_map(
        per_device,
        mesh=mesh,
        in_specs=(grid,) * 4
        + (media,) * 4
        + (P(), P(), P("shot"), P("shot", None), P("shot"), P("shot", None)),
        out_specs=P("shot", None, "gy", None),
        check_vma=False,
    )
```
